32 devices in a mesh: dp: 4 (over z), context: 4 (over y, core), tensor: 2 (over x).
Axes of the slice: x: 2, y: 2, z: 4, core: 2. Of those that a mesh axis runs over, the one named last changes fastest.
Arguments:
- inputs: bfloat16 [16, 1024, 1024], P('dp', 'context'), may hold values from -6 to 6
- lengths: int32 [16], P('dp'), may hold values from 256 to 1024
- query_weight: bfloat16 [1024, 1024], P('dp', 'tensor'), may hold values from -0.1875 to 0.1875
- key_weight: bfloat16 [1024, 512], P('dp', 'tensor'), may hold values from -0.1875 to 0.1875
- value_weight: bfloat16 [1024, 512], P('dp', 'tensor'), may hold values from -0.1875 to 0.1875
- out_weight: bfloat16 [1024, 1024], P('tensor', 'dp'), may hold values from -1 to 1
- gate_weight: bfloat16 [1024, 4608], P('dp', 'tensor'), may hold values from -0.1875 to 0.1875
- up_weight: bfloat16 [1024, 4608], P('dp', 'tensor'), may hold values from -0.1875 to 0.1875
- down_weight: bfloat16 [4608, 1024], P('tensor', 'dp'), may hold values from -0.09375 to 0.09375
- norm_gains: bfloat16 [2, 1024], P(None, 'dp'), may hold values from 0.25 to 1.75
- head_gains: bfloat16 [2, 64], P(None, 'dp'), may hold values from 0.25 to 1.75
- cotangent: bfloat16 [16, 1024, 1024], P('dp', 'context'), may hold values from -6 to 6
Outputs:
- outputs: bfloat16 [16, 1024, 1024], P('dp', 'context')
- input_grad: float32 [16, 1024, 1024], P('dp', 'context')
- query_weight_grad: float32 [1024, 1024], P('dp', 'tensor')
- key_weight_grad: float32 [1024, 512], P('dp', 'tensor')
- value_weight_grad: float32 [1024, 512], P('dp', 'tensor')
- out_weight_grad: float32 [1024, 1024], P('tensor', 'dp')
- gate_weight_grad: float32 [1024, 4608], P('dp', 'tensor')
- up_weight_grad: float32 [1024, 4608], P('dp', 'tensor')
- down_weight_grad: float32 [4608, 1024], P('tensor', 'dp')
- norm_gains_grad: float32 [2, 1024], P(None, 'dp')
- head_gains_grad: float32 [2, 64], P(None, 'dp')
The draws below stay inside these ranges and needn't reach their ends.
All inputs are finite; a program needn't handle non-finite values.
Results may differ from the reference program's by a relative error of at most 0.013.
Values may be sent and summed in bfloat16 or wider, within the bound.
A program may use at most 192 MiB of HBM per device.

```python
import jax
import jax.numpy as jnp
from jax import lax

D = 1024
HEADS = 16
KV_HEADS = 8
HD = 64
FF = 4608
SEQ = 1024
SEQ_DEV = 4
GROUP = 2
SEQS = 16
N_DP = 4


def set_ends(result, stream_key, low, top_value):
    longest = result.shape.index(max(result.shape))
    spots = []
    for shift in (0, 1):
        where = [jax.random.randint(jax.random.fold_in(stream_key, axis), (), 0, length) for axis, length in enumerate(result.shape)]
        where[longest] = (where[longest] + shift) % result.shape[longest]
        spots.append(tuple(where))
    return result.at[spots[0]].set(low).at[spots[1]].set(top_value)


def block_levels(own_key, shape, split, least, high):
    def one(position, shards_of):
        steps = jax.random.uniform(jax.random.fold_in(jax.random.fold_in(own_key, 6), position), (shards_of,), jnp.float32, least / len(split), high / len(split))
        return jnp.repeat(jnp.exp(steps), shape[position] // shards_of).reshape((-1,) + (1,) * (len(shape) - position - 1))

    factor_of = one(*split[0])
    for cut in split[1:]:
        factor_of = factor_of * one(*cut)
    return factor_of


def scatter_about(own_key, shape, deviation, reach, pieces=(), held_as=jnp.bfloat16):
    factor_of = block_levels(own_key, shape, pieces, -0.22, 0.18) if pieces else 1.0
    array = jax.random.normal(own_key, shape, jnp.float32) * deviation * factor_of
    return jnp.minimum(jnp.maximum(array, -reach), reach).astype(held_as)


def setup_inputs(seed: int = 0) -> dict:
    seeds = jax.random.split(jax.random.key(seed), 13)
    inputs = scatter_about(seeds[0], (SEQS, SEQ, D), 1.0, 6.0, ((0, 4), (1, 4)))
    lengths = set_ends(jax.random.randint(seeds[1], (SEQS,), SEQ // 4, SEQ + 1), jax.random.fold_in(seeds[1], 1), SEQ // 4, SEQ).astype(jnp.int32)
    query_weight = scatter_about(seeds[2], (D, HEADS * HD), D ** -0.5, 0.1875, ((0, 4), (1, 2)))
    key_weight = scatter_about(seeds[3], (D, KV_HEADS * HD), D ** -0.5, 0.1875, ((0, 4), (1, 2)))
    value_weight = scatter_about(seeds[4], (D, KV_HEADS * HD), D ** -0.5, 0.1875, ((0, 4), (1, 2)))
    out_weight = scatter_about(seeds[5], (HEADS * HD, D), 32 ** -0.5, 1.0, ((0, 2), (1, 4)))
    gate_weight = scatter_about(seeds[6], (D, FF), D ** -0.5, 0.1875, ((0, 4), (1, 2)))
    up_weight = scatter_about(seeds[7], (D, FF), D ** -0.5, 0.1875, ((0, 4), (1, 2)))
    down_weight = scatter_about(seeds[8], (FF, D), FF ** -0.5, 0.09375, ((0, 2), (1, 4)))
    norm_gains = jnp.clip(1.0 + 0.15 * jax.random.normal(seeds[9], (2, D), jnp.float32), 0.25, 1.75).astype(jnp.bfloat16)
    head_gains = jnp.clip(1.0 + 0.15 * jax.random.normal(seeds[10], (2, HD), jnp.float32), 0.25, 1.75).astype(jnp.bfloat16)
    cotangent = scatter_about(seeds[11], (SEQS, SEQ, D), 1.0, 6.0, ((0, 4), (1, 4)))
    return dict(inputs=inputs, lengths=lengths, query_weight=query_weight, key_weight=key_weight, value_weight=value_weight, out_weight=out_weight, gate_weight=gate_weight, up_weight=up_weight, down_weight=down_weight, norm_gains=norm_gains, head_gains=head_gains, cotangent=cotangent)


epsilon = 1e-05
rope_base = 1000000.0

@jax.custom_vjp
def low(v):
    return lax.optimization_barrier(v.astype(jnp.bfloat16)).astype(jnp.float32)

@jax.custom_vjp
def low_back(v):
    return v

def low_keep(v):
    return (low(v), None)

def low_pass(kept, grad):
    return (grad,)

def back_keep(v):
    return (v, None)

def back_low(kept, grad):
    return (low(grad),)
low.defvjp(low_keep, low_pass)
low_back.defvjp(back_keep, back_low)

def product(left_side, right_side):
    return jnp.matmul(left_side, right_side, precision=lax.Precision.HIGHEST)

def rms_norm(values):
    return values * lax.rsqrt(lax.optimization_barrier(jnp.mean(values * values, axis=-1, keepdims=True)) + epsilon)

def rotate(values, cosine_table, sine_table):
    half_width = values.shape[-1] // 2
    front_half = values[..., :half_width]
    back_half = values[..., half_width:]
    return jnp.concatenate([front_half * cosine_table - back_half * sine_table, back_half * cosine_table + front_half * sine_table], axis=-1)

def rope_tables(positions):
    half_width = HD // 2
    frequency = rope_base ** (-2.0 * jnp.arange(half_width, dtype=jnp.float32) / HD)
    angles = positions.astype(jnp.float32)[:, None] * frequency[None, :]
    return (jnp.cos(angles)[:, None, :], jnp.sin(angles)[:, None, :])

def attend(operands):
    queries, key_heads, values, length = operands
    positions = jnp.arange(SEQ, dtype=jnp.int32)
    grouped = queries.reshape(SEQ, KV_HEADS, GROUP, HD)
    scores = jnp.einsum('qkgd,skd->kgqs', grouped, key_heads, precision=lax.Precision.HIGHEST)
    scores = low_back(scores * HD ** (-0.5))
    allowed = (positions[None, :] <= positions[:, None]) & (positions[None, :] < length)
    scores = jnp.where(allowed, scores, -1e+30)
    weights = low(jax.nn.softmax(scores, axis=-1))
    mixed_heads = jnp.einsum('kgqs,skd->qkgd', weights, values, precision=lax.Precision.HIGHEST)
    return mixed_heads.reshape(SEQ, HEADS * HD)

def block_forward(params, inputs, lengths):
    query_weight, key_weight, value_weight, out_weight, gate_weight, up_weight, down_weight, norm_gains, head_gains = params
    batch_count = inputs.shape[0]
    cosine_table, sine_table = rope_tables(jnp.arange(SEQ, dtype=jnp.int32))
    normed = low(rms_norm(inputs) * norm_gains[0])
    queries = low_back(product(normed, query_weight)).reshape(batch_count, SEQ, HEADS, HD)
    key_heads = low_back(product(normed, key_weight)).reshape(batch_count, SEQ, KV_HEADS, HD)
    values = low(low_back(product(normed, value_weight))).reshape(batch_count, SEQ, KV_HEADS, HD)
    queries = low(rotate(rms_norm(queries) * head_gains[0], cosine_table, sine_table))
    key_heads = low(rotate(rms_norm(key_heads) * head_gains[1], cosine_table, sine_table))
    mixed_heads = lax.map(jax.checkpoint(attend), (queries, key_heads, values, lengths))
    mixed_heads = low(low_back(mixed_heads))
    attention = low_back(product(mixed_heads, out_weight))
    middle = inputs + attention
    normed_two = low(rms_norm(middle) * norm_gains[1])
    gate_proj = low_back(product(normed_two, gate_weight))
    up_proj = low_back(product(normed_two, up_weight))
    hidden = low(jax.nn.silu(gate_proj) * up_proj)
    return middle + low_back(product(hidden, down_weight))

def reference(inputs, lengths, query_weight, key_weight, value_weight, out_weight, gate_weight, up_weight, down_weight, norm_gains, head_gains, cotangent):
    params = tuple((matrix.astype(jnp.float32) for matrix in (query_weight, key_weight, value_weight, out_weight, gate_weight, up_weight, down_weight, norm_gains, head_gains)))
    zero_grads = tuple((jnp.zeros(matrix.shape, jnp.float32) for matrix in params))
    shaped_in = inputs.reshape(N_DP, SEQ_DEV, SEQ, D)
    shaped_len = lengths.reshape(N_DP, SEQ_DEV)
    shaped_cot = cotangent.reshape(N_DP, SEQ_DEV, SEQ, D)

    def scan_step(totals, group_data):
        block_in, block_len, block_cot = group_data
        positions = jnp.arange(SEQ, dtype=jnp.int32)
        live_mask = (positions[None, :] < block_len[:, None]).astype(jnp.float32)

        def forward(weights, values):
            return block_forward(weights, values, block_len)
        outputs, pullback = jax.vjp(forward, params, block_in.astype(jnp.float32))
        weight_grads, input_grad = pullback(block_cot.astype(jnp.float32) * live_mask[:, :, None])
        totals = jax.tree.map(lambda running, addend: running + addend, totals, weight_grads)
        return (totals, (outputs.astype(jnp.bfloat16), input_grad))
    totals, (outputs, input_grads) = lax.scan(scan_step, zero_grads, (shaped_in, shaped_len, shaped_cot))
    return (outputs.reshape(SEQS, SEQ, D), input_grads.reshape(SEQS, SEQ, D), totals[0], totals[1], totals[2], totals[3], totals[4], totals[5], totals[6], totals[7], totals[8])
```

```python
import functools

import jax
import jax.numpy as jnp
from jax import lax
from jax.experimental import pallas as pl
from jax.experimental.pallas import tpu as pltpu
from jax.sharding import PartitionSpec as P

HD = 64
ROWS = 256

epsilon = 1e-05
rope_base = 1000000.0

f32 = jnp.float32
bf16 = jnp.bfloat16

LANE_SWAP = [(0, 1), (1, 0), (2, 3), (3, 2)]
PAIR_SWAP = [(0, 2), (2, 0), (1, 3), (3, 1)]
SIDE_SWAP = [(0, 1), (1, 0)]
TURN = [(0, 0), (1, 2), (2, 1), (3, 3)]
TWIST_IN = [(0, 2), (1, 0), (2, 3), (3, 1)]
TWIST_OUT = [(b, a) for a, b in TWIST_IN]
CROSS = [(0, 0), (1, 2), (2, 1), (3, 3), (4, 4), (5, 6), (6, 5), (7, 7)]


def lane_swap(value):
    return lax.ppermute(value, "context", LANE_SWAP)


def pair_swap(value):
    return lax.ppermute(value, "context", PAIR_SWAP)


def side_swap(value):
    return lax.ppermute(value, "tensor", SIDE_SWAP)


def cross_swap(value):
    return lax.ppermute(value, ("context", "tensor"), CROSS)


def nn(left, right):
    return jnp.dot(left, right, preferred_element_type=f32)


def nt(left, right):
    return lax.dot_general(left, right, (((1,), (1,)), ((), ())), preferred_element_type=f32)


def tn(left, right):
    return lax.dot_general(left, right, (((0,), (0,)), ((), ())), preferred_element_type=f32)


def rms_scale(values):
    return lax.rsqrt(jnp.mean(values * values, axis=-1, keepdims=True) + epsilon)


def norm_back(upstream, normal, scale):
    return scale * (upstream - normal * jnp.mean(upstream * normal, axis=-1, keepdims=True))


def rope_tables(full_len):
    half_width = HD // 2
    frequency = rope_base ** (-2.0 * jnp.arange(half_width, dtype=f32) / HD)
    angles = jnp.arange(full_len, dtype=jnp.int32).astype(f32)[:, None] * frequency[None, :]
    cosine, sine = jnp.cos(angles), jnp.sin(angles)
    return (
        jnp.concatenate([cosine, cosine, cosine, cosine], axis=1),
        jnp.concatenate([-sine, sine, -sine, sine], axis=1),
    )


def head_ones():
    row = lax.broadcasted_iota(jnp.int32, (128, 128), 0) // HD
    column = lax.broadcasted_iota(jnp.int32, (128, 128), 1) // HD
    return (row == column).astype(bf16)


def head_sum(values, ones):
    high = values.astype(bf16)
    low = (values - high.astype(f32)).astype(bf16)
    return nn(high, ones) + nn(low, ones)


def half_turn(values):
    lane = lax.broadcasted_iota(jnp.int32, values.shape, 1)
    return jnp.where(lane % HD < HD // 2, pltpu.roll(values, 128 - HD // 2, 1), pltpu.roll(values, HD // 2, 1))


def attend_forward_kernel(
    table, qkv_ref, cos_ref, sin_ref, gain_ref, out_ref, inv_ref, qr_ref, kr_ref, vx_ref
):
    full_len = qkv_ref.shape[0]
    blocks = full_len // ROWS
    length = table[blocks]
    ones = head_ones()
    lane = lax.broadcasted_iota(jnp.int32, (ROWS, 128), 1)
    for block in range(blocks):
        local = pl.ds(pl.multiple_of(table[block] * ROWS, ROWS), ROWS)
        rows = slice(block * ROWS, (block + 1) * ROWS)
        cosine, sine = cos_ref[rows, :], sin_ref[rows, :]
        for part in range(3):
            value = qkv_ref[local, part * 128 : (part + 1) * 128]
            scale = lax.rsqrt(head_sum(value * value, ones) * (1.0 / HD) + epsilon)
            scaled = value * scale * gain_ref[min(part, 2) // 2 : min(part, 2) // 2 + 1, :]
            turned = (scaled * cosine + half_turn(scaled) * sine).astype(bf16)
            if part < 2:
                qr_ref[rows, part * 128 : (part + 1) * 128] = turned * HD ** (-0.5)
            else:
                kr_ref[rows, :] = turned
        value = qkv_ref[local, 384:512]
        position = block * ROWS + lax.broadcasted_iota(jnp.int32, (ROWS, 128), 0)
        valid = (position < length).astype(f32)
        value = value * valid
        vx_ref[0, rows, :] = jnp.where(lane < HD, value, valid).astype(bf16)
        vx_ref[1, rows, :] = jnp.where(lane < HD, pltpu.roll(value, HD, 1), valid).astype(bf16)
    for block in range(blocks):
        local = pl.ds(pl.multiple_of(table[block] * ROWS, ROWS), ROWS)
        rows = slice(block * ROWS, (block + 1) * ROWS)
        extent = (block + 1) * ROWS
        for head in range(2):
            query = jnp.concatenate(
                [
                    qr_ref[rows, head * 128 : head * 128 + HD],
                    qr_ref[rows, head * 128 + HD : head * 128 + 128],
                ],
                axis=0,
            )
            key = kr_ref[:extent, head * HD : (head + 1) * HD]
            scores = nt(query, key)
            total = None
            for piece in range(block + 1):
                weight = jnp.exp(scores[:, piece * ROWS : (piece + 1) * ROWS])
                if piece == block:
                    row = lax.broadcasted_iota(jnp.int32, weight.shape, 0) % ROWS
                    column = lax.broadcasted_iota(jnp.int32, weight.shape, 1)
                    weight = jnp.where(column <= row, weight, 0.0)
                term = nn(weight.astype(bf16), vx_ref[head, piece * ROWS : (piece + 1) * ROWS, :])
                total = term if total is None else total + term
            inverse = 1.0 / total
            mixed = total * pltpu.roll(inverse, HD, 1)
            first, second = mixed[:ROWS], mixed[ROWS:]
            inv_first, inv_second = inverse[:ROWS], inverse[ROWS:]
            columns = slice(head * 128, (head + 1) * 128)
            out_ref[local, columns] = jnp.where(lane < HD, first, pltpu.roll(second, HD, 1)).astype(bf16)
            inv_ref[local, columns] = jnp.where(lane < HD, pltpu.roll(inv_first, HD, 1), inv_second)


def attend_backward_kernel(
    table,
    qkv_ref,
    cos_ref,
    sin_ref,
    gain_ref,
    qr_ref,
    kr_ref,
    out_ref,
    inv_ref,
    grad_ref,
    dqkv_ref,
    dgain_ref,
    do_ref,
    vz_ref,
    kz_ref,
    dq_ref,
    dk_ref,
    dv_ref,
):
    full_len = qkv_ref.shape[0]
    blocks = full_len // ROWS
    length = table[blocks]
    ones = head_ones()
    dk_ref[...] = jnp.zeros_like(dk_ref)
    dv_ref[...] = jnp.zeros_like(dv_ref)
    for block in range(blocks):
        local = pl.ds(pl.multiple_of(table[block] * ROWS, ROWS), ROWS)
        rows = slice(block * ROWS, (block + 1) * ROWS)
        position = block * ROWS + lax.broadcasted_iota(jnp.int32, (ROWS, 128), 0)
        valid = (position < length).astype(f32)
        vz_ref[rows, :] = (qkv_ref[local, 384:512] * valid).astype(bf16)
        kz_ref[rows, :] = (kr_ref[rows, :].astype(f32) * valid).astype(bf16)
        do_ref[rows, :] = (grad_ref[local, :].astype(f32) * inv_ref[local, :]).astype(bf16)
    eight = jnp.ones((8, HD), bf16)
    for block in range(blocks):
        local = pl.ds(pl.multiple_of(table[block] * ROWS, ROWS), ROWS)
        rows = slice(block * ROWS, (block + 1) * ROWS)
        for head in range(2):
            low, mid, high = head * 128, head * 128 + HD, head * 128 + 128
            query = jnp.concatenate([qr_ref[rows, low:mid], qr_ref[rows, mid:high]], axis=0)
            upstream = jnp.concatenate([do_ref[rows, low:mid], do_ref[rows, mid:high]], axis=0)
            mixed = jnp.concatenate([out_ref[local, low:mid], out_ref[local, mid:high]], axis=0)
            product = upstream.astype(f32) * mixed.astype(f32)
            product_high = product.astype(bf16)
            product_low = (product - product_high.astype(f32)).astype(bf16)
            delta = (nt(eight, product_high) + nt(eight, product_low))[:1, :]
            dq_total = None
            for piece in range(block + 1):
                keys = slice(piece * ROWS, (piece + 1) * ROWS)
                half = slice(head * HD, (head + 1) * HD)
                weight = jnp.exp(nt(kr_ref[keys, half], query))
                if piece == block:
                    row = lax.broadcasted_iota(jnp.int32, weight.shape, 0)
                    column = lax.broadcasted_iota(jnp.int32, weight.shape, 1) % ROWS
                    weight = jnp.where(row <= column, weight, 0.0)
                score_grad = (weight * (nt(vz_ref[keys, half], upstream) - delta)).astype(bf16)
                dv_ref[head, keys, :] += nn(weight.astype(bf16), upstream)
                dk_ref[head, keys, :] += nn(score_grad, query)
                term = tn(score_grad, kz_ref[keys, half])
                dq_total = term if dq_total is None else dq_total + term
            dq_total = dq_total * HD ** (-0.5)
            dq_ref[rows, low:mid] = dq_total[:ROWS]
            dq_ref[rows, mid:high] = dq_total[ROWS:]
    gain_sums = [jnp.zeros((1, 128), f32) for _ in range(2)]
    for block in range(blocks):
        local = pl.ds(pl.multiple_of(table[block] * ROWS, ROWS), ROWS)
        rows = slice(block * ROWS, (block + 1) * ROWS)
        cosine, sine = cos_ref[rows, :], sin_ref[rows, :]
        position = block * ROWS + lax.broadcasted_iota(jnp.int32, (ROWS, 128), 0)
        valid = position < length
        for part in range(3):
            which = part // 2
            value = qkv_ref[local, part * 128 : (part + 1) * 128]
            scale = lax.rsqrt(head_sum(value * value, ones) * (1.0 / HD) + epsilon)
            normal = value * scale
            if part < 2:
                grad = dq_ref[rows, part * 128 : (part + 1) * 128]
            else:
                grad = jnp.concatenate([dk_ref[0, rows, :], dk_ref[1, rows, :]], axis=1)
                grad = jnp.where(valid, grad, 0.0)
            back = grad * cosine - half_turn(grad) * sine
            gain_sums[which] += jnp.sum(back * normal, axis=0, keepdims=True)
            scaled = back * gain_ref[which : which + 1, :]
            mean = head_sum(scaled * normal, ones) * (1.0 / HD)
            dqkv_ref[local, part * 128 : (part + 1) * 128] = (scale * (scaled - normal * mean)).astype(bf16)
        grad = jnp.concatenate([dv_ref[0, rows, :], dv_ref[1, rows, :]], axis=1)
        dqkv_ref[local, 384:512] = jnp.where(valid, grad, 0.0).astype(bf16)
    dgain_ref[0:1, :] = gain_sums[0]
    dgain_ref[1:2, :] = gain_sums[1]
    dgain_ref[2:8, :] = jnp.zeros((6, 128), f32)


def whole_spec():
    return pl.BlockSpec(memory_space=pltpu.VMEM)


def attend_forward(table, qkv, cosine, sine, gains):
    full_len = qkv.shape[0]
    return pl.pallas_call(
        attend_forward_kernel,
        out_shape=(
            jax.ShapeDtypeStruct((full_len, 256), bf16),
            jax.ShapeDtypeStruct((full_len, 256), f32),
            jax.ShapeDtypeStruct((full_len, 256), bf16),
            jax.ShapeDtypeStruct((full_len, 128), bf16),
        ),
        in_specs=[pl.BlockSpec(memory_space=pltpu.SMEM)] + [whole_spec()] * 4,
        out_specs=(whole_spec(),) * 4,
        scratch_shapes=[pltpu.VMEM((2, full_len, 128), bf16)],
        cost_estimate=pl.CostEstimate(flops=6 * 10**9, bytes_accessed=5 * 10**6, transcendentals=3 * 10**6),
    )(table, qkv, cosine, sine, gains)


def attend_backward(table, qkv, cosine, sine, gains, qr, kr, out, inverse, grad):
    full_len = qkv.shape[0]
    return pl.pallas_call(
        attend_backward_kernel,
        out_shape=(
            jax.ShapeDtypeStruct((full_len, 512), bf16),
            jax.ShapeDtypeStruct((8, 128), f32),
        ),
        in_specs=[pl.BlockSpec(memory_space=pltpu.SMEM)] + [whole_spec()] * 9,
        out_specs=(whole_spec(),) * 2,
        scratch_shapes=[
            pltpu.VMEM((full_len, 256), bf16),
            pltpu.VMEM((full_len, 128), bf16),
            pltpu.VMEM((full_len, 128), bf16),
            pltpu.VMEM((full_len, 256), f32),
            pltpu.VMEM((2, full_len, HD), f32),
            pltpu.VMEM((2, full_len, HD), f32),
        ],
        cost_estimate=pl.CostEstimate(flops=15 * 10**9, bytes_accessed=6 * 10**6, transcendentals=3 * 10**6),
    )(table, qkv, cosine, sine, gains, qr, kr, out, inverse, grad)


def cut(value, index, size, axis):
    return lax.dynamic_slice_in_dim(value, index * size, size, axis)


def pick(flag, first, second):
    return jnp.where(flag, first, second)


def spread(half, lane, side, out_dtype):
    block = half.shape[0] // 2
    first = lax.ppermute(half[:block], "context", TURN)
    second = lax.ppermute(half[block:], "context", TWIST_OUT)
    near = jnp.stack([first, second])
    far = side_swap(near)
    result = jnp.zeros((4,) + first.shape, out_dtype)
    for value, pair, other in ((near[0], 0, 0), (near[1], 1, 0), (far[0], 0, 1), (far[1], 1, 1)):
        place = 2 * lax.rem(lane + pair, 2) + lax.rem(side + other, 2)
        result = lax.dynamic_update_slice(result, value.astype(out_dtype)[None], (place, 0, 0))
    return result


def on_device(
    inputs,
    lengths,
    query_weight,
    key_weight,
    value_weight,
    out_weight,
    gate_weight,
    up_weight,
    down_weight,
    norm_gains,
    head_gains,
    cotangent,
):
    block_len, width = inputs.shape[1:]
    full_len = 4 * block_len
    context = lax.axis_index("context")
    pair, lane, side = context // 2, context % 2, lax.axis_index("tensor")
    owner = lax.axis_index("dp")
    shards = lax.axis_size("dp")
    shard = width // shards
    mine = 2 * pair + side

    q_cols, kv_cols, o_rows = query_weight.shape[1] // 2, key_weight.shape[1] // 2, out_weight.shape[0] // 2
    attn_shard = jnp.concatenate(
        [
            cut(query_weight, lane, q_cols, 1),
            cut(key_weight, lane, kv_cols, 1),
            cut(value_weight, lane, kv_cols, 1),
            cut(out_weight, lane, o_rows, 0).T,
        ],
        axis=1,
    )
    qkv_cols = q_cols + 2 * kv_cols
    attn_own = lax.all_gather(cross_swap(attn_shard), "dp", axis=0, tiled=True)
    qkv_own, out_own = attn_own[:, :qkv_cols], attn_own[:, qkv_cols:]
    qkv_far, out_far = side_swap(qkv_own), side_swap(out_own)

    gains_all = lax.all_gather(jnp.concatenate([norm_gains, head_gains], axis=1), "dp", axis=0)
    gains_full = gains_all[:, :, :shard].transpose(1, 0, 2).reshape(2, width).astype(f32)
    head_full = gains_all[:, :, shard:].transpose(1, 0, 2).reshape(2, HD).astype(f32)
    head_pair = jnp.concatenate([head_full, head_full], axis=1)
    gain_attn, gain_ffn = gains_full[0], gains_full[1]

    hidden = gate_weight.shape[1] // 2
    half_shard = shard // 2
    ffn_shard = jnp.concatenate(
        [
            cut(cut(gate_weight, lane, half_shard, 0), pair, hidden, 1),
            cut(cut(up_weight, lane, half_shard, 0), pair, hidden, 1),
            cut(cut(down_weight, lane, half_shard, 1), pair, hidden, 0).T,
        ],
        axis=1,
    )
    ffn_own = lax.all_gather(ffn_shard, "dp", axis=0, tiled=True).reshape(shards, half_shard, 3 * hidden)
    ffn_far = lane_swap(ffn_own)
    ffn_full = jnp.concatenate(
        [pick(lane == 0, ffn_own, ffn_far), pick(lane == 0, ffn_far, ffn_own)], axis=1
    ).reshape(width, 3 * hidden)
    gate_full, up_full, down_full = (
        ffn_full[:, :hidden],
        ffn_full[:, hidden : 2 * hidden],
        ffn_full[:, 2 * hidden :],
    )

    first_in = lax.ppermute(
        lax.dynamic_index_in_dim(inputs, 2 * lane + side, 0, False), "context", TURN
    )
    second_in = lax.ppermute(
        lax.dynamic_index_in_dim(inputs, 2 * (1 - lane) + side, 0, False), "context", TWIST_IN
    )
    x_half = jnp.concatenate([first_in, second_in], axis=0).astype(f32)
    half_len = x_half.shape[0]

    position = context * block_len + jnp.arange(block_len, dtype=jnp.int32)
    live = position[None, :] < lengths[:, None]
    upstream_low = jnp.where(live[:, :, None], cotangent, jnp.zeros((), bf16))
    up_first = lax.ppermute(upstream_low, "context", TURN)
    up_second = lax.ppermute(upstream_low, "context", TWIST_IN)

    def upstream_rows(sequence, turned):
        one = lax.dynamic_index_in_dim(up_first, sequence, 0, False)
        two = lax.dynamic_index_in_dim(up_second, sequence, 0, False)
        return jnp.concatenate([two, one] if turned else [one, two], axis=0)

    scale_one = rms_scale(x_half)
    normal_one = x_half * scale_one
    normed_half = (normal_one * gain_attn).astype(bf16)
    normed_one = jnp.concatenate([normed_half, lane_swap(normed_half)], axis=0)
    true_block = jnp.arange(4, dtype=jnp.int32)
    local_block = jnp.where(true_block // 2 == lane, 0, 2) + jnp.where(true_block % 2 == pair, 0, 1)
    table = jnp.concatenate([local_block, lax.dynamic_slice_in_dim(lengths, mine, 1)]).astype(jnp.int32)
    cosine, sine = rope_tables(full_len)
    qkv = [nn(normed_one, qkv_own), nn(normed_one, qkv_far)]
    mixed, inverse, q_rot, k_rot = zip(
        *[attend_forward(table, value, cosine, sine, head_pair) for value in qkv]
    )
    attn_part = nt(mixed[0], out_own) + nt(mixed[1], out_far)
    attn_recv = lane_swap(attn_part[half_len:].astype(bf16))
    middle = x_half + attn_part[:half_len] + attn_recv.astype(f32)
    scale_two = rms_scale(middle)
    normal_two = middle * scale_two
    normed_a = (normal_two * gain_ffn).astype(bf16)
    normed_b = side_swap(normed_a)
    normed_c = pair_swap(normed_a)
    normed_d = jnp.concatenate(
        [side_swap(normed_c[:block_len]), pair_swap(normed_b[block_len:])], axis=0
    )

    def feed_forward(normed, grad):
        gate_proj = nn(normed, gate_full)
        up_proj = nn(normed, up_full)
        hidden_grad = nn(grad, down_full)
        sigmoid_gate = jax.nn.sigmoid(gate_proj)
        silu_gate = gate_proj * sigmoid_gate
        hidden_low = (silu_gate * up_proj).astype(bf16)
        gate_grad = (
            hidden_grad * up_proj * sigmoid_gate * (1.0 + gate_proj * (1.0 - sigmoid_gate))
        ).astype(bf16)
        up_grad = (hidden_grad * silu_gate).astype(bf16)
        feed = nt(hidden_low, down_full)
        back = nt(gate_grad, gate_full) + nt(up_grad, up_full)
        return feed, back, hidden_low, gate_grad, up_grad

    far_pair = 2 * (1 - pair)
    grads = {
        "a": upstream_rows(mine, False),
        "b": upstream_rows(2 * pair + 1 - side, False),
        "c": upstream_rows(far_pair + side, True),
        "d": upstream_rows(far_pair + 1 - side, True),
    }
    normed = {"a": normed_a, "b": normed_b, "c": normed_c, "d": normed_d}
    done = {key: feed_forward(normed[key], grads[key]) for key in "abdc"}

    def gather_sum(which):
        part = {key: done[key][which] for key in "abcd"}
        low_d = part["d"].astype(bf16)
        from_side = side_swap(low_d[block_len:])
        from_pair = pair_swap(low_d[:block_len])
        send_b = jnp.concatenate(
            [part["b"][:block_len] + from_pair.astype(f32), part["b"][block_len:]], axis=0
        ).astype(bf16)
        send_c = jnp.concatenate(
            [part["c"][:block_len], part["c"][block_len:] + from_side.astype(f32)], axis=0
        ).astype(bf16)
        return part["a"] + side_swap(send_b).astype(f32) + pair_swap(send_c).astype(f32)

    back_two = gather_sum(1)
    normed_rows = jnp.concatenate([normed[key] for key in "abcd"], axis=0)
    grad_rows = jnp.concatenate([grads[key] for key in "abcd"], axis=0)
    hidden_rows = jnp.concatenate([done[key][2] for key in "abcd"], axis=0)
    gate_rows = jnp.concatenate([done[key][3] for key in "abcd"], axis=0)
    up_rows = jnp.concatenate([done[key][4] for key in "abcd"], axis=0)
    ffn_grad = jnp.concatenate(
        [tn(normed_rows, gate_rows), tn(normed_rows, up_rows), tn(grad_rows, hidden_rows)], axis=1
    ).reshape(shards, 2, half_shard, 3 * hidden)
    ffn_send = lax.dynamic_index_in_dim(ffn_grad, 1 - lane, 1, False).astype(bf16)
    ffn_keep = lax.dynamic_index_in_dim(ffn_grad, lane, 1, False)
    ffn_sum = (ffn_keep + lane_swap(ffn_send).astype(f32)).astype(bf16).reshape(shards * half_shard, 3 * hidden)
    ffn_piece = lax.psum_scatter(ffn_sum, "dp", scatter_dimension=0, tiled=True)
    ffn_pair = pair_swap(ffn_piece)
    both = jnp.concatenate([ffn_piece, ffn_pair], axis=1)
    both_far = lane_swap(both)
    low_rows, high_rows = pick(lane == 0, both, both_far), pick(lane == 0, both_far, both)
    rows_all = jnp.concatenate([low_rows, high_rows], axis=0).astype(f32)
    near_cols, far_cols = rows_all[:, : 3 * hidden], rows_all[:, 3 * hidden :]
    left, right = pick(pair == 0, near_cols, far_cols), pick(pair == 0, far_cols, near_cols)
    gate_shard, up_shard, down_turned = [
        jnp.concatenate(
            [left[:, i * hidden : (i + 1) * hidden], right[:, i * hidden : (i + 1) * hidden]], axis=1
        )
        for i in range(3)
    ]
    down_shard = down_turned.T

    feed_sum = gather_sum(0)
    out_half = (middle + feed_sum).astype(bf16)
    outputs = spread(out_half, lane, side, bf16)

    gain_ffn_grad = jnp.sum(back_two * normal_two, axis=0)
    middle_grad = grads["a"].astype(f32) + norm_back(back_two * gain_ffn, normal_two, scale_two)
    attn_low = middle_grad.astype(bf16)
    attn_grad = jnp.concatenate([attn_low, lane_swap(attn_low)], axis=0)
    weights = [(qkv_own, out_own), (qkv_far, out_far)]
    parts, back_one, gain_parts = [], None, 0.0
    for which in (1, 0):
        mixed_grad = nn(attn_grad, weights[which][1]).astype(bf16)
        qkv_grad, gain_part = attend_backward(
            table,
            qkv[which],
            cosine,
            sine,
            head_pair,
            q_rot[which],
            k_rot[which],
            mixed[which],
            inverse[which],
            mixed_grad,
        )
        parts.append(
            jnp.concatenate([tn(normed_one, qkv_grad), tn(attn_grad, mixed[which])], axis=1)
        )
        term = nt(qkv_grad, weights[which][0])
        back_one = term if back_one is None else back_one + term
        gain_parts = gain_parts + gain_part
    back_recv = lane_swap(back_one[half_len:].astype(bf16))
    back_half = back_one[:half_len] + back_recv.astype(f32)
    gain_attn_grad = jnp.sum(back_half * normal_one, axis=0)
    input_half = middle_grad + norm_back(back_half * gain_attn, normal_one, scale_one)
    input_grad = spread(input_half.astype(bf16), lane, side, f32)

    attn_sum = (parts[1] + side_swap(parts[0].astype(bf16)).astype(f32)).reshape(
        shards, 2, half_shard, qkv_cols + o_rows
    )
    attn_send = lax.dynamic_index_in_dim(attn_sum, 1 - pair, 1, False).astype(bf16)
    attn_keep = lax.dynamic_index_in_dim(attn_sum, pair, 1, False)
    attn_sum = (attn_keep + pair_swap(attn_send).astype(f32)).astype(bf16)
    attn_piece = lax.psum_scatter(
        attn_sum.reshape(shards * half_shard, qkv_cols + o_rows), "dp", scatter_dimension=0, tiled=True
    )
    attn_piece = cross_swap(attn_piece)
    piece_pair = pair_swap(attn_piece)
    columns = jnp.concatenate(
        [pick(pair == 0, attn_piece, piece_pair), pick(pair == 0, piece_pair, attn_piece)], axis=0
    )
    columns_far = lane_swap(columns)
    left = pick(lane == 0, columns, columns_far).astype(f32)
    right = pick(lane == 0, columns_far, columns).astype(f32)
    query_shard = jnp.concatenate([left[:, :q_cols], right[:, :q_cols]], axis=1)
    key_shard = jnp.concatenate(
        [left[:, q_cols : q_cols + kv_cols], right[:, q_cols : q_cols + kv_cols]], axis=1
    )
    value_shard = jnp.concatenate(
        [left[:, q_cols + kv_cols : qkv_cols], right[:, q_cols + kv_cols : qkv_cols]], axis=1
    )
    out_shard = jnp.concatenate([left[:, qkv_cols:].T, right[:, qkv_cols:].T], axis=0)

    head_grad = gain_parts[:2, :HD] + gain_parts[:2, HD:]
    gain_total = lax.psum(
        jnp.concatenate([jnp.stack([gain_attn_grad, gain_ffn_grad]), head_grad], axis=1),
        ("dp", "context", "tensor"),
    )
    gain_shard = cut(gain_total[:, :width], owner, shard, 1)
    head_shard = cut(gain_total[:, width:], owner, HD // shards, 1)
    return (
        outputs,
        input_grad,
        query_shard,
        key_shard,
        value_shard,
        out_shard,
        gate_shard,
        up_shard,
        down_shard,
        gain_shard,
        head_shard,
    )


def solution(mesh):
    in_specs = (
        P("dp", "context", None),
        P("dp"),
        P("dp", "tensor"),
        P("dp", "tensor"),
        P("dp", "tensor"),
        P("tensor", "dp"),
        P("dp", "tensor"),
        P("dp", "tensor"),
        P("tensor", "dp"),
        P(None, "dp"),
        P(None, "dp"),
        P("dp", "context", None),
    )
    out_specs = (
        P("dp", "context", None),
        P("dp", "context", None),
        P("dp", "tensor"),
        P("dp", "tensor"),
        P("dp", "tensor"),
        P("tensor", "dp"),
        P("dp", "tensor"),
        P("dp", "tensor"),
        P("tensor", "dp"),
        P(None, "dp"),
        P(None, "dp"),
    )
    return jax.shard_map(
        on_device, mesh=mesh, in_specs=in_specs, out_specs=out_specs, check_vma=False
    )
```

```python
import functools

import jax
import jax.numpy as jnp
from jax import lax
from jax.experimental import pallas as pl
from jax.experimental.layout import Layout, with_layout_constraint
from jax.experimental.pallas import tpu as pltpu
from jax.sharding import PartitionSpec as P

HD = 64
ROWS = 256

epsilon = 1e-05
rope_base = 1000000.0

f32 = jnp.float32
bf16 = jnp.bfloat16

LANE_SWAP = [(0, 1), (1, 0), (2, 3), (3, 2)]
PAIR_SWAP = [(0, 2), (2, 0), (1, 3), (3, 1)]
SIDE_SWAP = [(0, 1), (1, 0)]
TURN = [(1, 2), (2, 1)]
TWIST_IN = [(0, 2), (1, 0), (2, 3), (3, 1)]
TWIST_OUT = [(b, a) for a, b in TWIST_IN]
CROSS = [(1, 2), (2, 1), (5, 6), (6, 5)]


def lane_swap(value):
    return lax.ppermute(value, "context", LANE_SWAP)


def pair_swap(value):
    return lax.ppermute(value, "context", PAIR_SWAP)


def side_swap(value):
    return lax.ppermute(value, "tensor", SIDE_SWAP)


def cross_swap(value, lane, side):
    moved = lax.ppermute(value, ("context", "tensor"), CROSS)
    return jnp.where(lane == side, value, moved)


def turn(value, pair, lane):
    moved = lax.ppermute(value, "context", TURN)
    return jnp.where(pair == lane, value, moved)


def after(value, *others):
    return lax.optimization_barrier((value,) + others)[0]


def row_major(value):
    return with_layout_constraint(value, Layout(tuple(range(value.ndim))))


def nn(left, right):
    return jnp.dot(left, right, preferred_element_type=f32)


def nt(left, right):
    return lax.dot_general(left, right, (((1,), (1,)), ((), ())), preferred_element_type=f32)


def tn(left, right):
    return lax.dot_general(left, right, (((0,), (0,)), ((), ())), preferred_element_type=f32)


def rms_scale(values):
    return lax.rsqrt(jnp.mean(values * values, axis=-1, keepdims=True) + epsilon)


def norm_back(upstream, normal, scale):
    return scale * (upstream - normal * jnp.mean(upstream * normal, axis=-1, keepdims=True))


def rope_tables(full_len):
    half_width = HD // 2
    frequency = rope_base ** (-2.0 * jnp.arange(half_width, dtype=f32) / HD)
    angles = jnp.arange(full_len, dtype=jnp.int32).astype(f32)[:, None] * frequency[None, :]
    cosine, sine = jnp.cos(angles), jnp.sin(angles)
    return (
        jnp.concatenate([cosine, cosine, cosine, cosine], axis=1),
        jnp.concatenate([-sine, sine, -sine, sine], axis=1),
    )


def head_ones():
    row = lax.broadcasted_iota(jnp.int32, (128, 128), 0) // HD
    column = lax.broadcasted_iota(jnp.int32, (128, 128), 1) // HD
    return (row == column).astype(bf16)


def head_sum(values, ones):
    high = values.astype(bf16)
    low = (values - high.astype(f32)).astype(bf16)
    return nn(high, ones) + nn(low, ones)


def half_turn(values):
    lane = lax.broadcasted_iota(jnp.int32, values.shape, 1)
    return jnp.where(lane % HD < HD // 2, pltpu.roll(values, 128 - HD // 2, 1), pltpu.roll(values, HD // 2, 1))


def attend_forward_kernel(
    table, qkv_ref, cos_ref, sin_ref, gain_ref, out_ref, inv_ref, qr_ref, kr_ref, vx_ref
):
    full_len = qkv_ref.shape[0]
    blocks = full_len // ROWS
    length = table[blocks]
    ones = head_ones()
    lane = lax.broadcasted_iota(jnp.int32, (ROWS, 128), 1)
    for block in range(blocks):
        local = pl.ds(pl.multiple_of(table[block] * ROWS, ROWS), ROWS)
        rows = slice(block * ROWS, (block + 1) * ROWS)
        cosine, sine = cos_ref[rows, :], sin_ref[rows, :]
        for part in range(3):
            value = qkv_ref[local, part * 128 : (part + 1) * 128]
            scale = lax.rsqrt(head_sum(value * value, ones) * (1.0 / HD) + epsilon)
            scaled = value * scale * gain_ref[min(part, 2) // 2 : min(part, 2) // 2 + 1, :]
            turned = (scaled * cosine + half_turn(scaled) * sine).astype(bf16)
            if part < 2:
                qr_ref[rows, part * 128 : (part + 1) * 128] = turned * HD ** (-0.5)
            else:
                kr_ref[rows, :] = turned
        value = qkv_ref[local, 384:512]
        position = block * ROWS + lax.broadcasted_iota(jnp.int32, (ROWS, 128), 0)
        valid = (position < length).astype(f32)
        value = value * valid
        vx_ref[0, rows, :] = jnp.where(lane < HD, value, valid).astype(bf16)
        vx_ref[1, rows, :] = jnp.where(lane < HD, pltpu.roll(value, HD, 1), valid).astype(bf16)
    for block in range(blocks):
        local = pl.ds(pl.multiple_of(table[block] * ROWS, ROWS), ROWS)
        rows = slice(block * ROWS, (block + 1) * ROWS)
        extent = (block + 1) * ROWS
        for head in range(2):
            query = jnp.concatenate(
                [
                    qr_ref[rows, head * 128 : head * 128 + HD],
                    qr_ref[rows, head * 128 + HD : head * 128 + 128],
                ],
                axis=0,
            )
            key = kr_ref[:extent, head * HD : (head + 1) * HD]
            scores = nt(query, key)
            total = None
            for piece in range(block + 1):
                weight = jnp.exp(scores[:, piece * ROWS : (piece + 1) * ROWS])
                if piece == block:
                    row = lax.broadcasted_iota(jnp.int32, weight.shape, 0) % ROWS
                    column = lax.broadcasted_iota(jnp.int32, weight.shape, 1)
                    weight = jnp.where(column <= row, weight, 0.0)
                term = nn(weight.astype(bf16), vx_ref[head, piece * ROWS : (piece + 1) * ROWS, :])
                total = term if total is None else total + term
            inverse = 1.0 / total
            mixed = total * pltpu.roll(inverse, HD, 1)
            first, second = mixed[:ROWS], mixed[ROWS:]
            inv_first, inv_second = inverse[:ROWS], inverse[ROWS:]
            columns = slice(head * 128, (head + 1) * 128)
            out_ref[local, columns] = jnp.where(lane < HD, first, pltpu.roll(second, HD, 1)).astype(bf16)
            inv_ref[local, columns] = jnp.where(lane < HD, pltpu.roll(inv_first, HD, 1), inv_second)


def attend_backward_kernel(
    table,
    qkv_ref,
    cos_ref,
    sin_ref,
    gain_ref,
    qr_ref,
    kr_ref,
    out_ref,
    inv_ref,
    grad_ref,
    dqkv_ref,
    dgain_ref,
    do_ref,
    vz_ref,
    kz_ref,
    dq_ref,
    dk_ref,
    dv_ref,
):
    full_len = qkv_ref.shape[0]
    blocks = full_len // ROWS
    length = table[blocks]
    ones = head_ones()
    dk_ref[...] = jnp.zeros_like(dk_ref)
    dv_ref[...] = jnp.zeros_like(dv_ref)
    for block in range(blocks):
        local = pl.ds(pl.multiple_of(table[block] * ROWS, ROWS), ROWS)
        rows = slice(block * ROWS, (block + 1) * ROWS)
        position = block * ROWS + lax.broadcasted_iota(jnp.int32, (ROWS, 128), 0)
        valid = (position < length).astype(f32)
        vz_ref[rows, :] = (qkv_ref[local, 384:512] * valid).astype(bf16)
        kz_ref[rows, :] = (kr_ref[rows, :].astype(f32) * valid).astype(bf16)
        do_ref[rows, :] = (grad_ref[local, :].astype(f32) * inv_ref[local, :]).astype(bf16)
    eight = jnp.ones((8, HD), bf16)
    for block in range(blocks):
        local = pl.ds(pl.multiple_of(table[block] * ROWS, ROWS), ROWS)
        rows = slice(block * ROWS, (block + 1) * ROWS)
        for head in range(2):
            low, mid, high = head * 128, head * 128 + HD, head * 128 + 128
            query = jnp.concatenate([qr_ref[rows, low:mid], qr_ref[rows, mid:high]], axis=0)
            upstream = jnp.concatenate([do_ref[rows, low:mid], do_ref[rows, mid:high]], axis=0)
            mixed = jnp.concatenate([out_ref[local, low:mid], out_ref[local, mid:high]], axis=0)
            product = upstream.astype(f32) * mixed.astype(f32)
            product_high = product.astype(bf16)
            product_low = (product - product_high.astype(f32)).astype(bf16)
            delta = (nt(eight, product_high) + nt(eight, product_low))[:1, :]
            dq_total = None
            for piece in range(block + 1):
                keys = slice(piece * ROWS, (piece + 1) * ROWS)
                half = slice(head * HD, (head + 1) * HD)
                weight = jnp.exp(nt(kr_ref[keys, half], query))
                if piece == block:
                    row = lax.broadcasted_iota(jnp.int32, weight.shape, 0)
                    column = lax.broadcasted_iota(jnp.int32, weight.shape, 1) % ROWS
                    weight = jnp.where(row <= column, weight, 0.0)
                score_grad = (weight * (nt(vz_ref[keys, half], upstream) - delta)).astype(bf16)
                dv_ref[head, keys, :] += nn(weight.astype(bf16), upstream)
                dk_ref[head, keys, :] += nn(score_grad, query)
                term = tn(score_grad, kz_ref[keys, half])
                dq_total = term if dq_total is None else dq_total + term
            dq_total = dq_total * HD ** (-0.5)
            dq_ref[rows, low:mid] = dq_total[:ROWS]
            dq_ref[rows, mid:high] = dq_total[ROWS:]
    gain_sums = [jnp.zeros((1, 128), f32) for _ in range(2)]
    for block in range(blocks):
        local = pl.ds(pl.multiple_of(table[block] * ROWS, ROWS), ROWS)
        rows = slice(block * ROWS, (block + 1) * ROWS)
        cosine, sine = cos_ref[rows, :], sin_ref[rows, :]
        position = block * ROWS + lax.broadcasted_iota(jnp.int32, (ROWS, 128), 0)
        valid = position < length
        for part in range(3):
            which = part // 2
            value = qkv_ref[local, part * 128 : (part + 1) * 128]
            scale = lax.rsqrt(head_sum(value * value, ones) * (1.0 / HD) + epsilon)
            normal = value * scale
            if part < 2:
                grad = dq_ref[rows, part * 128 : (part + 1) * 128]
            else:
                grad = jnp.concatenate([dk_ref[0, rows, :], dk_ref[1, rows, :]], axis=1)
                grad = jnp.where(valid, grad, 0.0)
            back = grad * cosine - half_turn(grad) * sine
            gain_sums[which] += jnp.sum(back * normal, axis=0, keepdims=True)
            scaled = back * gain_ref[which : which + 1, :]
            mean = head_sum(scaled * normal, ones) * (1.0 / HD)
            dqkv_ref[local, part * 128 : (part + 1) * 128] = (scale * (scaled - normal * mean)).astype(bf16)
        grad = jnp.concatenate([dv_ref[0, rows, :], dv_ref[1, rows, :]], axis=1)
        dqkv_ref[local, 384:512] = jnp.where(valid, grad, 0.0).astype(bf16)
    dgain_ref[0:1, :] = gain_sums[0]
    dgain_ref[1:2, :] = gain_sums[1]
    dgain_ref[2:8, :] = jnp.zeros((6, 128), f32)


def whole_spec():
    return pl.BlockSpec(memory_space=pltpu.VMEM)


def attend_forward(table, qkv, cosine, sine, gains):
    full_len = qkv.shape[0]
    return pl.pallas_call(
        attend_forward_kernel,
        out_shape=(
            jax.ShapeDtypeStruct((full_len, 256), bf16),
            jax.ShapeDtypeStruct((full_len, 256), f32),
            jax.ShapeDtypeStruct((full_len, 256), bf16),
            jax.ShapeDtypeStruct((full_len, 128), bf16),
        ),
        in_specs=[pl.BlockSpec(memory_space=pltpu.SMEM)] + [whole_spec()] * 4,
        out_specs=(whole_spec(),) * 4,
        scratch_shapes=[pltpu.VMEM((2, full_len, 128), bf16)],
        cost_estimate=pl.CostEstimate(flops=10**9, bytes_accessed=10**6, transcendentals=0),
    )(table, qkv, cosine, sine, gains)


def attend_backward(table, qkv, cosine, sine, gains, qr, kr, out, inverse, grad):
    full_len = qkv.shape[0]
    return pl.pallas_call(
        attend_backward_kernel,
        out_shape=(
            jax.ShapeDtypeStruct((full_len, 512), bf16),
            jax.ShapeDtypeStruct((8, 128), f32),
        ),
        in_specs=[pl.BlockSpec(memory_space=pltpu.SMEM)] + [whole_spec()] * 9,
        out_specs=(whole_spec(),) * 2,
        scratch_shapes=[
            pltpu.VMEM((full_len, 256), bf16),
            pltpu.VMEM((full_len, 128), bf16),
            pltpu.VMEM((full_len, 128), bf16),
            pltpu.VMEM((full_len, 256), f32),
            pltpu.VMEM((2, full_len, HD), f32),
            pltpu.VMEM((2, full_len, HD), f32),
        ],
        cost_estimate=pl.CostEstimate(flops=2 * 10**9, bytes_accessed=10**6, transcendentals=0),
    )(table, qkv, cosine, sine, gains, qr, kr, out, inverse, grad)


def feed_forward_kernel(
    shards,
    turned,
    table,
    normed_ref,
    first_ref,
    second_ref,
    own_ref,
    far_ref,
    feed_ref,
    back_ref,
    hidden_ref,
    gate_grad_ref,
    up_grad_ref,
    weight_ref,
    sems,
):
    step = pl.program_id(0)
    lane = lax.rem(lax.axis_index("context"), 2)
    width, columns = weight_ref.shape
    hidden = columns // 3
    half_shard = width // shards // 2
    parts = [slice(0, hidden), slice(hidden, 2 * hidden), slice(2 * hidden, 3 * hidden)]

    def copies(part):
        found = []
        for owner in range(shards):
            source = pl.ds(owner * half_shard, half_shard)
            for far, ref in ((0, own_ref), (1, far_ref)):
                place = (2 * owner + (1 - lane if far else lane)) * half_shard
                found.append(
                    pltpu.make_async_copy(
                        ref.at[source, parts[part]],
                        weight_ref.at[pl.ds(pl.multiple_of(place, half_shard), half_shard), parts[part]],
                        sems.at[part, 2 * owner + far],
                    )
                )
        return found

    @pl.when(step == 0)
    def _():
        for part in range(3):
            for copy in copies(part):
                copy.start()

    def ready(part):
        @pl.when(step == 0)
        def _():
            for copy in copies(part):
                copy.wait()

    normed = normed_ref[...]
    use_first = (step == 0) != turned
    grad = jnp.where(use_first, first_ref[0], second_ref[0])
    ready(0)
    gate_proj = nn(normed, weight_ref[:, parts[0]])
    ready(1)
    up_proj = nn(normed, weight_ref[:, parts[1]])
    ready(2)
    hidden_grad = nn(grad, weight_ref[:, parts[2]])
    sigmoid_gate = 1.0 / (1.0 + jnp.exp(-gate_proj))
    silu_gate = gate_proj * sigmoid_gate
    hidden_low = (silu_gate * up_proj).astype(bf16)
    gate_grad = (
        hidden_grad * up_proj * (sigmoid_gate + silu_gate * (1.0 - sigmoid_gate))
    ).astype(bf16)
    up_grad = (hidden_grad * silu_gate).astype(bf16)
    hidden_ref[...] = hidden_low
    gate_grad_ref[...] = gate_grad
    up_grad_ref[...] = up_grad
    back = nt(gate_grad, weight_ref[:, parts[0]]) + nt(up_grad, weight_ref[:, parts[1]])
    back_ref[...] = back.astype(back_ref.dtype)
    feed_ref[...] = nt(hidden_low, weight_ref[:, parts[2]]).astype(feed_ref.dtype)


def feed_forward(sequence, turned, out_dtype, shards, normed, up_first, up_second, own, far):
    rows, width = normed.shape
    tile = rows // 2
    columns = own.shape[1]
    hidden = columns // 3
    grad_spec = pl.BlockSpec((1, tile, width), lambda i, t: (t[0], 0, 0))
    return pl.pallas_call(
        functools.partial(feed_forward_kernel, shards, turned),
        grid_spec=pltpu.PrefetchScalarGridSpec(
            num_scalar_prefetch=1,
            grid=(2,),
            in_specs=[
                pl.BlockSpec((tile, width), lambda i, t: (i, 0)),
                grad_spec,
                grad_spec,
                pl.BlockSpec(memory_space=pl.ANY),
                pl.BlockSpec(memory_space=pl.ANY),
            ],
            out_specs=[
                pl.BlockSpec((tile, width), lambda i, t: (i, 0)),
                pl.BlockSpec((tile, width), lambda i, t: (i, 0)),
                pl.BlockSpec((tile, hidden), lambda i, t: (i, 0)),
                pl.BlockSpec((tile, hidden), lambda i, t: (i, 0)),
                pl.BlockSpec((tile, hidden), lambda i, t: (i, 0)),
            ],
            scratch_shapes=[
                pltpu.VMEM((width, columns), bf16),
                pltpu.SemaphoreType.DMA((3, 2 * shards)),
            ],
        ),
        out_shape=[
            jax.ShapeDtypeStruct((rows, width), out_dtype),
            jax.ShapeDtypeStruct((rows, width), out_dtype),
            jax.ShapeDtypeStruct((rows, hidden), bf16),
            jax.ShapeDtypeStruct((rows, hidden), bf16),
            jax.ShapeDtypeStruct((rows, hidden), bf16),
        ],
        cost_estimate=pl.CostEstimate(
            flops=rows * width * hidden, bytes_accessed=10**6, transcendentals=0
        ),
    )(sequence[None], normed, up_first, up_second, own, far)


def store_halves(which, shards, total_ref, near_ref, far_ref):
    half = total_ref.shape[0] // shards // 2
    for owner in range(shards):
        rows = slice(owner * half, (owner + 1) * half)
        near = pl.ds(pl.multiple_of((2 * owner + which) * half, half), half)
        far = pl.ds(pl.multiple_of((2 * owner + 1 - which) * half, half), half)
        near_ref[rows, :] = total_ref[near, :].astype(bf16)
        far_ref[rows, :] = total_ref[far, :].astype(bf16)


def left_grad_kernel(shards, *refs):
    lefts, rights = refs[:4], refs[4:8]
    near_ref, far_ref, total_ref = refs[8:]
    lane = lax.rem(lax.axis_index("context"), 2)
    total_ref[...] = sum(tn(left[...], right[...]) for left, right in zip(lefts, rights))
    store_halves(lane, shards, total_ref, near_ref, far_ref)


def left_grad(shards, lefts, rights):
    rows, width = lefts[0].shape
    hidden = rights[0].shape[1]
    tile = hidden // 3
    half = width // 2
    return pl.pallas_call(
        functools.partial(left_grad_kernel, shards),
        grid=(3,),
        in_specs=[pl.BlockSpec((rows, width), lambda j: (0, 0))] * 4
        + [pl.BlockSpec((rows, tile), lambda j: (0, j))] * 4,
        out_specs=[pl.BlockSpec((half, tile), lambda j: (0, j))] * 2,
        out_shape=[jax.ShapeDtypeStruct((half, hidden), bf16)] * 2,
        scratch_shapes=[pltpu.VMEM((width, tile), f32)],
        cost_estimate=pl.CostEstimate(
            flops=rows * width * hidden, bytes_accessed=10**6, transcendentals=0
        ),
    )(*lefts, *rights)


def down_grad_kernel(shards, table, first_ref, second_ref, *refs):
    rights = refs[:4]
    near_ref, far_ref, total_ref = refs[4:]
    lane = lax.rem(lax.axis_index("context"), 2)
    tile = first_ref.shape[1]
    total = None
    for index, right in enumerate(rights):
        order = (first_ref, second_ref) if index < 2 else (second_ref, first_ref)
        for part, left in enumerate(order):
            term = tn(left[table[index]], right[part * tile : (part + 1) * tile, :])
            total = term if total is None else total + term
    total_ref[...] = total
    store_halves(lane, shards, total_ref, near_ref, far_ref)


def down_grad(shards, sequences, up_first, up_second, rights):
    rows, hidden = rights[0].shape
    width = up_first.shape[2]
    tile = hidden // 3
    half = width // 2
    whole = pl.BlockSpec(up_first.shape, lambda j, t: (0, 0, 0))
    return pl.pallas_call(
        functools.partial(down_grad_kernel, shards),
        grid_spec=pltpu.PrefetchScalarGridSpec(
            num_scalar_prefetch=1,
            grid=(3,),
            in_specs=[whole, whole] + [pl.BlockSpec((rows, tile), lambda j, t: (0, j))] * 4,
            out_specs=[pl.BlockSpec((half, tile), lambda j, t: (0, j))] * 2,
            scratch_shapes=[pltpu.VMEM((width, tile), f32)],
        ),
        out_shape=[jax.ShapeDtypeStruct((half, hidden), bf16)] * 2,
        cost_estimate=pl.CostEstimate(
            flops=rows * width * hidden, bytes_accessed=10**6, transcendentals=0
        ),
    )(sequences, up_first, up_second, *rights)


def attn_grad_kernel(shards, normed_ref, grad_ref, upstream_ref, mixed_ref, near_ref, far_ref, total_ref):
    pair = lax.axis_index("context") // 2
    columns = grad_ref.shape[1]
    total_ref[:, :columns] = tn(normed_ref[...], grad_ref[...])
    total_ref[:, columns:] = tn(upstream_ref[...], mixed_ref[...])
    store_halves(pair, shards, total_ref, near_ref, far_ref)


def attn_weight_grad(shards, normed, grad, upstream, mixed):
    width = normed.shape[1]
    columns = grad.shape[1] + mixed.shape[1]
    return pl.pallas_call(
        functools.partial(attn_grad_kernel, shards),
        in_specs=[whole_spec()] * 4,
        out_specs=[whole_spec()] * 2,
        out_shape=[jax.ShapeDtypeStruct((width // 2, columns), bf16)] * 2,
        scratch_shapes=[pltpu.VMEM((width, columns), f32)],
        cost_estimate=pl.CostEstimate(
            flops=10**8, bytes_accessed=10**6, transcendentals=0
        ),
    )(normed, grad, upstream, mixed)


def join_ffn_kernel(pieces, outs):
    context = lax.axis_index("context")
    pair, lane = context // 2, lax.rem(context, 2)
    gate_ref, up_ref, down_ref = outs
    half, columns = pieces[0][0].shape
    hidden = columns // 3
    for row in range(2):
        for column in range(2):
            for part in range(3):
                cols = slice(part * hidden, (part + 1) * hidden)
                values = [
                    jnp.where(pair == column, pieces[a][0][:, cols], pieces[a][1][:, cols])
                    for a in range(2)
                ]
                value = jnp.where(lane == row, values[0], values[1]).astype(f32)
                rows = slice(row * half, (row + 1) * half)
                into = slice(column * hidden, (column + 1) * hidden)
                if part == 2:
                    down_ref[into, rows] = value.T
                else:
                    (gate_ref, up_ref)[part][rows, into] = value


def join_ffn(near, near_pair, far, far_pair):
    half, columns = near.shape
    hidden = columns // 3

    def kernel(a, b, c, d, *outs):
        join_ffn_kernel([[a, b], [c, d]], outs)

    return pl.pallas_call(
        kernel,
        in_specs=[whole_spec()] * 4,
        out_specs=[whole_spec()] * 3,
        out_shape=[
            jax.ShapeDtypeStruct((2 * half, 2 * hidden), f32),
            jax.ShapeDtypeStruct((2 * half, 2 * hidden), f32),
            jax.ShapeDtypeStruct((2 * hidden, 2 * half), f32),
        ],
        cost_estimate=pl.CostEstimate(flops=10**6, bytes_accessed=10**6, transcendentals=0),
    )(near, near_pair, far, far_pair)


def join_attn(q_cols, kv_cols, near, near_pair, far, far_pair):
    half, columns = near.shape
    o_rows = columns - q_cols - 2 * kv_cols
    cuts = [
        slice(0, q_cols),
        slice(q_cols, q_cols + kv_cols),
        slice(q_cols + kv_cols, q_cols + 2 * kv_cols),
        slice(q_cols + 2 * kv_cols, columns),
    ]

    def kernel(a, b, c, d, q_ref, k_ref, v_ref, o_ref):
        context = lax.axis_index("context")
        pair, lane = context // 2, lax.rem(context, 2)
        for column in range(2):
            for row in range(2):
                rows = slice(row * half, (row + 1) * half)
                for part, cols in enumerate(cuts):
                    one = jnp.where(pair == row, a[:, cols], b[:, cols])
                    two = jnp.where(pair == row, c[:, cols], d[:, cols])
                    value = jnp.where(lane == column, one, two).astype(f32)
                    wide = cols.stop - cols.start
                    into = slice(column * wide, (column + 1) * wide)
                    if part == 3:
                        o_ref[into, rows] = value.T
                    else:
                        (q_ref, k_ref, v_ref)[part][rows, into] = value

    return pl.pallas_call(
        kernel,
        in_specs=[whole_spec()] * 4,
        out_specs=[whole_spec()] * 4,
        out_shape=[
            jax.ShapeDtypeStruct((2 * half, 2 * q_cols), f32),
            jax.ShapeDtypeStruct((2 * half, 2 * kv_cols), f32),
            jax.ShapeDtypeStruct((2 * half, 2 * kv_cols), f32),
            jax.ShapeDtypeStruct((2 * o_rows, 2 * half), f32),
        ],
        cost_estimate=pl.CostEstimate(flops=10**6, bytes_accessed=2 * 10**6, transcendentals=0),
    )(near, near_pair, far, far_pair)


def join_rows(places, values, out_dtype):
    block, width = values[0].shape

    def kernel(table, a, b, c, d, out_ref):
        for index, ref in enumerate((a, b, c, d)):

            @pl.when(table[index] == pl.program_id(0))
            def _():
                out_ref[0] = ref[...].astype(out_dtype)

    return pl.pallas_call(
        kernel,
        grid_spec=pltpu.PrefetchScalarGridSpec(
            num_scalar_prefetch=1,
            grid=(4,),
            in_specs=[pl.BlockSpec((block, width), lambda i, t: (0, 0))] * 4,
            out_specs=pl.BlockSpec((1, block, width), lambda i, t: (i, 0, 0)),
        ),
        out_shape=jax.ShapeDtypeStruct((4, block, width), out_dtype),
        cost_estimate=pl.CostEstimate(flops=10**6, bytes_accessed=10**6, transcendentals=0),
    )(places, *values)


def cut(value, index, size, axis):
    return lax.dynamic_slice_in_dim(value, index * size, size, axis)


def spread(first_rows, second_rows, pair, lane, side, out_dtype):
    first = turn(first_rows, pair, lane)
    second = lax.ppermute(second_rows, "context", TWIST_OUT)
    values = [first, second, side_swap(first), side_swap(second)]
    places = jnp.stack(
        [2 * lane + side, 2 * (1 - lane) + side, 2 * lane + 1 - side, 2 * (1 - lane) + 1 - side]
    ).astype(jnp.int32)
    return join_rows(places, values, out_dtype)


def on_device(
    inputs,
    lengths,
    query_weight,
    key_weight,
    value_weight,
    out_weight,
    gate_weight,
    up_weight,
    down_weight,
    norm_gains,
    head_gains,
    cotangent,
):
    block_len, width = inputs.shape[1:]
    full_len = 4 * block_len
    context = lax.axis_index("context")
    pair, lane, side = context // 2, context % 2, lax.axis_index("tensor")
    owner = lax.axis_index("dp")
    shards = lax.axis_size("dp")
    shard = width // shards
    half_shard = shard // 2
    mine = 2 * pair + side

    q_cols, kv_cols, o_rows = query_weight.shape[1] // 2, key_weight.shape[1] // 2, out_weight.shape[0] // 2
    attn_shard = row_major(
        jnp.concatenate(
            [
                cut(query_weight, lane, q_cols, 1),
                cut(key_weight, lane, kv_cols, 1),
                cut(value_weight, lane, kv_cols, 1),
                cut(out_weight, lane, o_rows, 0).T,
            ],
            axis=1,
        )
    )
    qkv_cols = q_cols + 2 * kv_cols
    attn_own = lax.all_gather(row_major(cross_swap(attn_shard, lane, side)), "dp", axis=0, tiled=True)
    qkv_own, out_own = row_major(attn_own[:, :qkv_cols]), row_major(attn_own[:, qkv_cols:])
    qkv_far, out_far = row_major(side_swap(qkv_own)), row_major(side_swap(out_own))

    gains_all = lax.all_gather(jnp.concatenate([norm_gains, head_gains], axis=1), "dp", axis=0)
    gains_full = gains_all[:, :, :shard].transpose(1, 0, 2).reshape(2, width).astype(f32)
    head_full = gains_all[:, :, shard:].transpose(1, 0, 2).reshape(2, HD).astype(f32)
    head_pair = jnp.concatenate([head_full, head_full], axis=1)
    gain_attn, gain_ffn = gains_full[0], gains_full[1]

    hidden = gate_weight.shape[1] // 2
    ffn_shard = row_major(
        jnp.concatenate(
            [
                cut(cut(gate_weight, lane, half_shard, 0), pair, hidden, 1),
                cut(cut(up_weight, lane, half_shard, 0), pair, hidden, 1),
                cut(cut(down_weight, lane, half_shard, 1), pair, hidden, 0).T,
            ],
            axis=1,
        )
    )
    ffn_own = row_major(lax.all_gather(ffn_shard, "dp", axis=0, tiled=True))

    first_in = turn(
        lax.dynamic_index_in_dim(inputs, 2 * lane + side, 0, False), pair, lane
    )
    second_in = lax.ppermute(
        lax.dynamic_index_in_dim(inputs, 2 * (1 - lane) + side, 0, False), "context", TWIST_IN
    )
    x_half = jnp.concatenate([first_in, second_in], axis=0).astype(f32)
    half_len = x_half.shape[0]

    position = context * block_len + jnp.arange(block_len, dtype=jnp.int32)
    live = position[None, :] < lengths[:, None]
    upstream_low = jnp.where(live[:, :, None], cotangent, jnp.zeros((), bf16))
    upstream_low = after(upstream_low, first_in, second_in)
    up_first = turn(upstream_low, pair, lane)
    up_second = lax.ppermute(upstream_low, "context", TWIST_IN)

    scale_one = rms_scale(x_half)
    normal_one = x_half * scale_one
    normed_half = (normal_one * gain_attn).astype(bf16)
    normed_one = jnp.concatenate([normed_half, lane_swap(normed_half)], axis=0)
    true_block = jnp.arange(4, dtype=jnp.int32)
    local_block = jnp.where(true_block // 2 == lane, 0, 2) + jnp.where(true_block % 2 == pair, 0, 1)
    table = jnp.concatenate([local_block, lax.dynamic_slice_in_dim(lengths, mine, 1)]).astype(jnp.int32)
    cosine, sine = rope_tables(full_len)
    qkv = [nn(normed_one, qkv_own), nn(normed_one, qkv_far)]
    qkv[1] = after(qkv[1], up_first, up_second)
    mixed, inverse, q_rot, k_rot = zip(
        *[attend_forward(table, value, cosine, sine, head_pair) for value in qkv]
    )
    attn_part = nt(mixed[0], out_own) + nt(mixed[1], out_far)
    attn_recv = lane_swap(attn_part[half_len:].astype(bf16))
    middle = x_half + attn_part[:half_len] + attn_recv.astype(f32)
    scale_two = rms_scale(middle)
    normal_two = middle * scale_two
    normed_a = (normal_two * gain_ffn).astype(bf16)
    ffn_own = after(ffn_own, normed_a)
    ffn_far = row_major(lane_swap(ffn_own))
    normed_b = side_swap(normed_a)
    normed_c = pair_swap(normed_a)

    far_pair = 2 * (1 - pair)
    sequences = jnp.stack(
        [mine, 2 * pair + 1 - side, far_pair + side, far_pair + 1 - side]
    ).astype(jnp.int32)

    def run(index, normed, out_dtype):
        return feed_forward(
            sequences[index], index >= 2, out_dtype, shards, normed, up_first, up_second, ffn_own, ffn_far
        )

    done_a = run(0, normed_a, f32)
    normed_b, normed_c = after(normed_b, done_a[0]), after(normed_c, done_a[0])
    normed_d = jnp.concatenate(
        [side_swap(normed_c[:block_len]), pair_swap(normed_b[block_len:])], axis=0
    )
    done_b = run(1, normed_b, bf16)
    done_d = run(3, after(normed_d, done_b[0]), bf16)
    done_c = run(2, after(normed_c, done_d[0]), bf16)

    def first_stage(which):
        return side_swap(done_d[which][block_len:]), pair_swap(done_d[which][:block_len])

    def second_stage(which, from_side, from_pair):
        b, c = done_b[which], done_c[which]
        send_b = jnp.concatenate([b[:block_len] + from_pair, b[block_len:]], axis=0)
        send_c = jnp.concatenate([c[:block_len], c[block_len:] + from_side], axis=0)
        return send_b, send_c

    back_from = first_stage(1)
    rights = [(done_a, done_b, done_c, done_d)[i][2] for i in range(4)]
    down_near, down_far = down_grad(shards, sequences, up_first, up_second, rights)
    send_b, send_c = second_stage(1, *back_from)
    back_b, back_c = side_swap(send_b), pair_swap(send_c)
    lefts = [normed_a, normed_b, normed_c, normed_d]
    lefts[0] = after(normed_a, send_b, send_c, down_near)
    gates = [(done_a, done_b, done_c, done_d)[i][3] for i in range(4)]
    ups = [(done_a, done_b, done_c, done_d)[i][4] for i in range(4)]
    gate_near, gate_far = left_grad(shards, lefts, gates)
    lefts[0] = after(lefts[0], gate_near)
    up_near, up_far = left_grad(shards, lefts, ups)
    ffn_sum = jnp.concatenate(
        [
            gate_near + lane_swap(gate_far),
            up_near + lane_swap(up_far),
            down_near + lane_swap(down_far),
        ],
        axis=1,
    )
    ffn_piece = row_major(lax.psum_scatter(row_major(ffn_sum), "dp", scatter_dimension=0, tiled=True))
    ffn_pair = pair_swap(ffn_piece)
    gate_shard, up_shard, down_shard = join_ffn(
        ffn_piece, ffn_pair, lane_swap(ffn_piece), lane_swap(ffn_pair)
    )

    upstream = jnp.concatenate(
        [
            lax.dynamic_index_in_dim(up_first, mine, 0, False),
            lax.dynamic_index_in_dim(up_second, mine, 0, False),
        ],
        axis=0,
    ).astype(f32)
    back_two = done_a[1] + back_b.astype(f32) + back_c.astype(f32)
    gain_ffn_grad = jnp.sum(back_two * normal_two, axis=0)
    middle_grad = upstream + norm_back(back_two * gain_ffn, normal_two, scale_two)
    feed_from = first_stage(0)
    send_b, send_c = second_stage(0, *feed_from)
    send_b, send_c = after(send_b, back_two), after(send_c, back_two)
    feed_sum = done_a[0] + side_swap(send_b).astype(f32) + pair_swap(send_c).astype(f32)
    out_half = (middle + feed_sum).astype(bf16)

    attn_low = after(middle_grad.astype(bf16), up_near)
    attn_grad = jnp.concatenate([attn_low, lane_swap(attn_low)], axis=0)
    weights = [(qkv_own, out_own), (qkv_far, out_far)]
    pieces, back_one, gain_parts = {}, None, 0.0
    for which in (1, 0):
        mixed_grad = nn(attn_grad, weights[which][1]).astype(bf16)
        if which == 0:
            mixed_grad = after(mixed_grad, pieces[1][0], send_b, send_c)
        qkv_grad, gain_part = attend_backward(
            table,
            qkv[which],
            cosine,
            sine,
            head_pair,
            q_rot[which],
            k_rot[which],
            mixed[which],
            inverse[which],
            mixed_grad,
        )
        pieces[which] = attn_weight_grad(shards, normed_one, qkv_grad, attn_grad, mixed[which])
        term = nt(qkv_grad, weights[which][0])
        back_one = term if back_one is None else back_one + term
        gain_parts = gain_parts + gain_part
    back_recv = lane_swap(back_one[half_len:].astype(bf16))
    back_half = back_one[:half_len] + back_recv.astype(f32)
    gain_attn_grad = jnp.sum(back_half * normal_one, axis=0)
    outputs = spread(out_half[:block_len], out_half[block_len:], pair, lane, side, bf16)
    back_half = after(back_half, out_half)
    input_half = (middle_grad + norm_back(back_half * gain_attn, normal_one, scale_one)).astype(bf16)
    input_grad = spread(input_half[:block_len], input_half[block_len:], pair, lane, side, f32)

    near, far = (mine_part + side_swap(other) for mine_part, other in zip(pieces[0], pieces[1]))
    attn_sum = row_major(near + pair_swap(far))
    attn_piece = row_major(lax.psum_scatter(attn_sum, "dp", scatter_dimension=0, tiled=True))
    attn_piece = cross_swap(attn_piece, lane, side)
    piece_pair = pair_swap(attn_piece)
    query_shard, key_shard, value_shard, out_shard = join_attn(
        q_cols, kv_cols, attn_piece, piece_pair, lane_swap(attn_piece), lane_swap(piece_pair)
    )

    head_grad = gain_parts[:2, :HD] + gain_parts[:2, HD:]
    gain_total = jnp.concatenate([jnp.stack([gain_attn_grad, gain_ffn_grad]), head_grad], axis=1)
    gain_total = gain_total + lane_swap(gain_total)
    gain_total = gain_total + side_swap(gain_total)
    gain_total = gain_total + pair_swap(gain_total)
    hop = 1
    while hop < shards:
        pairs = [(i, i ^ hop) for i in range(shards)]
        gain_total = gain_total + lax.ppermute(gain_total, "dp", pairs)
        hop *= 2
    gain_shard = cut(gain_total[:, :width], owner, shard, 1)
    head_shard = cut(gain_total[:, width:], owner, HD // shards, 1)
    return (
        outputs,
        input_grad,
        query_shard,
        key_shard,
        value_shard,
        out_shard,
        gate_shard,
        up_shard,
        down_shard,
        gain_shard,
        head_shard,
    )


def solution(mesh):
    in_specs = (
        P("dp", "context", None),
        P("dp"),
        P("dp", "tensor"),
        P("dp", "tensor"),
        P("dp", "tensor"),
        P("tensor", "dp"),
        P("dp", "tensor"),
        P("dp", "tensor"),
        P("tensor", "dp"),
        P(None, "dp"),
        P(None, "dp"),
        P("dp", "context", None),
    )
    out_specs = (
        P("dp", "context", None),
        P("dp", "context", None),
        P("dp", "tensor"),
        P("dp", "tensor"),
        P("dp", "tensor"),
        P("tensor", "dp"),
        P("dp", "tensor"),
        P("dp", "tensor"),
        P("tensor", "dp"),
        P(None, "dp"),
        P(None, "dp"),
    )
    return jax.shard_map(
        on_device, mesh=mesh, in_specs=in_specs, out_specs=out_specs, check_vma=False
    )
```

```python
import functools

import jax
import jax.numpy as jnp
from jax import lax
from jax.experimental import pallas as pl
from jax.experimental.layout import Layout, with_layout_constraint
from jax.experimental.pallas import tpu as pltpu
from jax.sharding import PartitionSpec as P

HD = 64
ROWS = 256

epsilon = 1e-05
rope_base = 1000000.0

f32 = jnp.float32
bf16 = jnp.bfloat16

LANE_SWAP = [(0, 1), (1, 0), (2, 3), (3, 2)]
PAIR_SWAP = [(0, 2), (2, 0), (1, 3), (3, 1)]
SIDE_SWAP = [(0, 1), (1, 0)]
TURN = [(1, 2), (2, 1)]
TWIST_IN = [(0, 2), (1, 0), (2, 3), (3, 1)]
TWIST_OUT = [(b, a) for a, b in TWIST_IN]
CROSS = [(1, 2), (2, 1), (5, 6), (6, 5)]


def lane_swap(value):
    return lax.ppermute(value, "context", LANE_SWAP)


def pair_swap(value):
    return lax.ppermute(value, "context", PAIR_SWAP)


def side_swap(value):
    return lax.ppermute(value, "tensor", SIDE_SWAP)


def cross_swap(value, lane, side):
    moved = lax.ppermute(value, ("context", "tensor"), CROSS)
    return jnp.where(lane == side, value, moved)


def turn(value, pair, lane):
    moved = lax.ppermute(value, "context", TURN)
    return jnp.where(pair == lane, value, moved)


def after(value, *others):
    return lax.optimization_barrier((value,) + others)[0]


def row_major(value):
    return with_layout_constraint(value, Layout(tuple(range(value.ndim))))


def nn(left, right):
    return jnp.dot(left, right, preferred_element_type=f32)


def nt(left, right):
    return lax.dot_general(left, right, (((1,), (1,)), ((), ())), preferred_element_type=f32)


def tn(left, right):
    return lax.dot_general(left, right, (((0,), (0,)), ((), ())), preferred_element_type=f32)


def rms_scale(values):
    return lax.rsqrt(jnp.mean(values * values, axis=-1, keepdims=True) + epsilon)


def norm_back(upstream, normal, scale):
    return scale * (upstream - normal * jnp.mean(upstream * normal, axis=-1, keepdims=True))


def rope_tables(full_len):
    half_width = HD // 2
    frequency = rope_base ** (-2.0 * jnp.arange(half_width, dtype=f32) / HD)
    angles = jnp.arange(full_len, dtype=jnp.int32).astype(f32)[:, None] * frequency[None, :]
    cosine, sine = jnp.cos(angles), jnp.sin(angles)
    return (
        jnp.concatenate([cosine, cosine, cosine, cosine], axis=1),
        jnp.concatenate([-sine, sine, -sine, sine], axis=1),
    )


def head_ones():
    row = lax.broadcasted_iota(jnp.int32, (128, 128), 0) // HD
    column = lax.broadcasted_iota(jnp.int32, (128, 128), 1) // HD
    return (row == column).astype(bf16)


def head_sum(values, ones):
    high = values.astype(bf16)
    low = (values - high.astype(f32)).astype(bf16)
    return nn(high, ones) + nn(low, ones)


def half_turn(values):
    lane = lax.broadcasted_iota(jnp.int32, values.shape, 1)
    return jnp.where(lane % HD < HD // 2, pltpu.roll(values, 128 - HD // 2, 1), pltpu.roll(values, HD // 2, 1))


def attend_forward_kernel(
    table, qkv_ref, cos_ref, sin_ref, gain_ref, out_ref, inv_ref, qr_ref, kr_ref, vx_ref
):
    full_len = qkv_ref.shape[0]
    blocks = full_len // ROWS
    length = table[blocks]
    ones = head_ones()
    lane = lax.broadcasted_iota(jnp.int32, (ROWS, 128), 1)
    for block in range(blocks):
        local = pl.ds(pl.multiple_of(table[block] * ROWS, ROWS), ROWS)
        rows = slice(block * ROWS, (block + 1) * ROWS)
        cosine, sine = cos_ref[rows, :], sin_ref[rows, :]
        for part in range(3):
            value = qkv_ref[local, part * 128 : (part + 1) * 128]
            scale = lax.rsqrt(head_sum(value * value, ones) * (1.0 / HD) + epsilon)
            scaled = value * scale * gain_ref[min(part, 2) // 2 : min(part, 2) // 2 + 1, :]
            turned = (scaled * cosine + half_turn(scaled) * sine).astype(bf16)
            if part < 2:
                qr_ref[rows, part * 128 : (part + 1) * 128] = turned * HD ** (-0.5)
            else:
                kr_ref[rows, :] = turned
        value = qkv_ref[local, 384:512]
        position = block * ROWS + lax.broadcasted_iota(jnp.int32, (ROWS, 128), 0)
        valid = (position < length).astype(f32)
        value = value * valid
        vx_ref[0, rows, :] = jnp.where(lane < HD, value, valid).astype(bf16)
        vx_ref[1, rows, :] = jnp.where(lane < HD, pltpu.roll(value, HD, 1), valid).astype(bf16)
    for block in range(blocks):
        local = pl.ds(pl.multiple_of(table[block] * ROWS, ROWS), ROWS)
        rows = slice(block * ROWS, (block + 1) * ROWS)
        extent = (block + 1) * ROWS
        for head in range(2):
            query = jnp.concatenate(
                [
                    qr_ref[rows, head * 128 : head * 128 + HD],
                    qr_ref[rows, head * 128 + HD : head * 128 + 128],
                ],
                axis=0,
            )
            key = kr_ref[:extent, head * HD : (head + 1) * HD]
            scores = nt(query, key)
            total = None
            for piece in range(block + 1):
                weight = jnp.exp(scores[:, piece * ROWS : (piece + 1) * ROWS])
                if piece == block:
                    row = lax.broadcasted_iota(jnp.int32, weight.shape, 0) % ROWS
                    column = lax.broadcasted_iota(jnp.int32, weight.shape, 1)
                    weight = jnp.where(column <= row, weight, 0.0)
                term = nn(weight.astype(bf16), vx_ref[head, piece * ROWS : (piece + 1) * ROWS, :])
                total = term if total is None else total + term
            inverse = 1.0 / total
            mixed = total * pltpu.roll(inverse, HD, 1)
            first, second = mixed[:ROWS], mixed[ROWS:]
            inv_first, inv_second = inverse[:ROWS], inverse[ROWS:]
            columns = slice(head * 128, (head + 1) * 128)
            out_ref[local, columns] = jnp.where(lane < HD, first, pltpu.roll(second, HD, 1)).astype(bf16)
            inv_ref[local, columns] = jnp.where(lane < HD, pltpu.roll(inv_first, HD, 1), inv_second)


def attend_backward_kernel(
    table,
    qkv_ref,
    cos_ref,
    sin_ref,
    gain_ref,
    qr_ref,
    kr_ref,
    out_ref,
    inv_ref,
    grad_ref,
    dqkv_ref,
    dgain_ref,
    do_ref,
    vz_ref,
    kz_ref,
    dq_ref,
    dk_ref,
    dv_ref,
):
    full_len = qkv_ref.shape[0]
    blocks = full_len // ROWS
    length = table[blocks]
    ones = head_ones()
    dk_ref[...] = jnp.zeros_like(dk_ref)
    dv_ref[...] = jnp.zeros_like(dv_ref)
    for block in range(blocks):
        local = pl.ds(pl.multiple_of(table[block] * ROWS, ROWS), ROWS)
        rows = slice(block * ROWS, (block + 1) * ROWS)
        position = block * ROWS + lax.broadcasted_iota(jnp.int32, (ROWS, 128), 0)
        valid = (position < length).astype(f32)
        vz_ref[rows, :] = (qkv_ref[local, 384:512] * valid).astype(bf16)
        kz_ref[rows, :] = (kr_ref[rows, :].astype(f32) * valid).astype(bf16)
        do_ref[rows, :] = (grad_ref[local, :].astype(f32) * inv_ref[local, :]).astype(bf16)
    eight = jnp.ones((8, HD), bf16)
    for block in range(blocks):
        local = pl.ds(pl.multiple_of(table[block] * ROWS, ROWS), ROWS)
        rows = slice(block * ROWS, (block + 1) * ROWS)
        for head in range(2):
            low, mid, high = head * 128, head * 128 + HD, head * 128 + 128
            query = jnp.concatenate([qr_ref[rows, low:mid], qr_ref[rows, mid:high]], axis=0)
            upstream = jnp.concatenate([do_ref[rows, low:mid], do_ref[rows, mid:high]], axis=0)
            mixed = jnp.concatenate([out_ref[local, low:mid], out_ref[local, mid:high]], axis=0)
            product = upstream.astype(f32) * mixed.astype(f32)
            product_high = product.astype(bf16)
            product_low = (product - product_high.astype(f32)).astype(bf16)
            delta = (nt(eight, product_high) + nt(eight, product_low))[:1, :]
            dq_total = None
            for piece in range(block + 1):
                keys = slice(piece * ROWS, (piece + 1) * ROWS)
                half = slice(head * HD, (head + 1) * HD)
                weight = jnp.exp(nt(kr_ref[keys, half], query))
                if piece == block:
                    row = lax.broadcasted_iota(jnp.int32, weight.shape, 0)
                    column = lax.broadcasted_iota(jnp.int32, weight.shape, 1) % ROWS
                    weight = jnp.where(row <= column, weight, 0.0)
                score_grad = (weight * (nt(vz_ref[keys, half], upstream) - delta)).astype(bf16)
                dv_ref[head, keys, :] += nn(weight.astype(bf16), upstream)
                dk_ref[head, keys, :] += nn(score_grad, query)
                term = tn(score_grad, kz_ref[keys, half])
                dq_total = term if dq_total is None else dq_total + term
            dq_total = dq_total * HD ** (-0.5)
            dq_ref[rows, low:mid] = dq_total[:ROWS]
            dq_ref[rows, mid:high] = dq_total[ROWS:]
    gain_sums = [jnp.zeros((1, 128), f32) for _ in range(2)]
    for block in range(blocks):
        local = pl.ds(pl.multiple_of(table[block] * ROWS, ROWS), ROWS)
        rows = slice(block * ROWS, (block + 1) * ROWS)
        cosine, sine = cos_ref[rows, :], sin_ref[rows, :]
        position = block * ROWS + lax.broadcasted_iota(jnp.int32, (ROWS, 128), 0)
        valid = position < length
        for part in range(3):
            which = part // 2
            value = qkv_ref[local, part * 128 : (part + 1) * 128]
            scale = lax.rsqrt(head_sum(value * value, ones) * (1.0 / HD) + epsilon)
            normal = value * scale
            if part < 2:
                grad = dq_ref[rows, part * 128 : (part + 1) * 128]
            else:
                grad = jnp.concatenate([dk_ref[0, rows, :], dk_ref[1, rows, :]], axis=1)
                grad = jnp.where(valid, grad, 0.0)
            back = grad * cosine - half_turn(grad) * sine
            gain_sums[which] += jnp.sum(back * normal, axis=0, keepdims=True)
            scaled = back * gain_ref[which : which + 1, :]
            mean = head_sum(scaled * normal, ones) * (1.0 / HD)
            dqkv_ref[local, part * 128 : (part + 1) * 128] = (scale * (scaled - normal * mean)).astype(bf16)
        grad = jnp.concatenate([dv_ref[0, rows, :], dv_ref[1, rows, :]], axis=1)
        dqkv_ref[local, 384:512] = jnp.where(valid, grad, 0.0).astype(bf16)
    dgain_ref[0:1, :] = gain_sums[0]
    dgain_ref[1:2, :] = gain_sums[1]
    dgain_ref[2:8, :] = jnp.zeros((6, 128), f32)


def whole_spec():
    return pl.BlockSpec(memory_space=pltpu.VMEM)


def attend_forward(table, qkv, cosine, sine, gains):
    full_len = qkv.shape[0]
    return pl.pallas_call(
        attend_forward_kernel,
        out_shape=(
            jax.ShapeDtypeStruct((full_len, 256), bf16),
            jax.ShapeDtypeStruct((full_len, 256), f32),
            jax.ShapeDtypeStruct((full_len, 256), bf16),
            jax.ShapeDtypeStruct((full_len, 128), bf16),
        ),
        in_specs=[pl.BlockSpec(memory_space=pltpu.SMEM)] + [whole_spec()] * 4,
        out_specs=(whole_spec(),) * 4,
        scratch_shapes=[pltpu.VMEM((2, full_len, 128), bf16)],
        cost_estimate=pl.CostEstimate(flops=10**9, bytes_accessed=10**6, transcendentals=0),
    )(table, qkv, cosine, sine, gains)


def attend_backward(table, qkv, cosine, sine, gains, qr, kr, out, inverse, grad):
    full_len = qkv.shape[0]
    return pl.pallas_call(
        attend_backward_kernel,
        out_shape=(
            jax.ShapeDtypeStruct((full_len, 512), bf16),
            jax.ShapeDtypeStruct((8, 128), f32),
        ),
        in_specs=[pl.BlockSpec(memory_space=pltpu.SMEM)] + [whole_spec()] * 9,
        out_specs=(whole_spec(),) * 2,
        scratch_shapes=[
            pltpu.VMEM((full_len, 256), bf16),
            pltpu.VMEM((full_len, 128), bf16),
            pltpu.VMEM((full_len, 128), bf16),
            pltpu.VMEM((full_len, 256), f32),
            pltpu.VMEM((2, full_len, HD), f32),
            pltpu.VMEM((2, full_len, HD), f32),
        ],
        cost_estimate=pl.CostEstimate(flops=2 * 10**9, bytes_accessed=10**6, transcendentals=0),
    )(table, qkv, cosine, sine, gains, qr, kr, out, inverse, grad)


def feed_forward_kernel(
    shards,
    turned,
    table,
    normed_ref,
    first_ref,
    second_ref,
    own_ref,
    far_ref,
    feed_ref,
    back_ref,
    hidden_ref,
    gate_grad_ref,
    up_grad_ref,
    weight_ref,
    sems,
):
    step = pl.program_id(0)
    lane = lax.rem(lax.axis_index("context"), 2)
    width, columns = weight_ref.shape
    hidden = columns // 3
    half_shard = width // shards // 2
    parts = [slice(0, hidden), slice(hidden, 2 * hidden), slice(2 * hidden, 3 * hidden)]

    def copies(part):
        found = []
        for owner in range(shards):
            source = pl.ds(owner * half_shard, half_shard)
            for far, ref in ((0, own_ref), (1, far_ref)):
                place = (2 * owner + (1 - lane if far else lane)) * half_shard
                found.append(
                    pltpu.make_async_copy(
                        ref.at[source, parts[part]],
                        weight_ref.at[pl.ds(pl.multiple_of(place, half_shard), half_shard), parts[part]],
                        sems.at[part, 2 * owner + far],
                    )
                )
        return found

    @pl.when(step == 0)
    def _():
        for part in range(3):
            for copy in copies(part):
                copy.start()

    def ready(part):
        @pl.when(step == 0)
        def _():
            for copy in copies(part):
                copy.wait()

    normed = normed_ref[...]
    use_first = (step == 0) != turned
    grad = jnp.where(use_first, first_ref[0], second_ref[0])
    ready(0)
    gate_proj = nn(normed, weight_ref[:, parts[0]])
    ready(1)
    up_proj = nn(normed, weight_ref[:, parts[1]])
    ready(2)
    hidden_grad = nn(grad, weight_ref[:, parts[2]])
    sigmoid_gate = 1.0 / (1.0 + jnp.exp(-gate_proj))
    silu_gate = gate_proj * sigmoid_gate
    hidden_low = (silu_gate * up_proj).astype(bf16)
    gate_grad = (
        hidden_grad * up_proj * (sigmoid_gate + silu_gate * (1.0 - sigmoid_gate))
    ).astype(bf16)
    up_grad = (hidden_grad * silu_gate).astype(bf16)
    hidden_ref[...] = hidden_low
    gate_grad_ref[...] = gate_grad
    up_grad_ref[...] = up_grad
    back = nt(gate_grad, weight_ref[:, parts[0]]) + nt(up_grad, weight_ref[:, parts[1]])
    back_ref[...] = back.astype(back_ref.dtype)
    feed_ref[...] = nt(hidden_low, weight_ref[:, parts[2]]).astype(feed_ref.dtype)


def feed_forward(sequence, turned, out_dtype, shards, normed, up_first, up_second, own, far):
    rows, width = normed.shape
    tile = rows // 2
    columns = own.shape[1]
    hidden = columns // 3
    grad_spec = pl.BlockSpec((1, tile, width), lambda i, t: (t[0], 0, 0))
    return pl.pallas_call(
        functools.partial(feed_forward_kernel, shards, turned),
        grid_spec=pltpu.PrefetchScalarGridSpec(
            num_scalar_prefetch=1,
            grid=(2,),
            in_specs=[
                pl.BlockSpec((tile, width), lambda i, t: (i, 0)),
                grad_spec,
                grad_spec,
                pl.BlockSpec(memory_space=pl.ANY),
                pl.BlockSpec(memory_space=pl.ANY),
            ],
            out_specs=[
                pl.BlockSpec((tile, width), lambda i, t: (i, 0)),
                pl.BlockSpec((tile, width), lambda i, t: (i, 0)),
                pl.BlockSpec((tile, hidden), lambda i, t: (i, 0)),
                pl.BlockSpec((tile, hidden), lambda i, t: (i, 0)),
                pl.BlockSpec((tile, hidden), lambda i, t: (i, 0)),
            ],
            scratch_shapes=[
                pltpu.VMEM((width, columns), bf16),
                pltpu.SemaphoreType.DMA((3, 2 * shards)),
            ],
        ),
        out_shape=[
            jax.ShapeDtypeStruct((rows, width), out_dtype),
            jax.ShapeDtypeStruct((rows, width), out_dtype),
            jax.ShapeDtypeStruct((rows, hidden), bf16),
            jax.ShapeDtypeStruct((rows, hidden), bf16),
            jax.ShapeDtypeStruct((rows, hidden), bf16),
        ],
        cost_estimate=pl.CostEstimate(
            flops=rows * width * hidden, bytes_accessed=10**6, transcendentals=0
        ),
    )(sequence[None], normed, up_first, up_second, own, far)


def store_halves(which, shards, total_ref, near_ref, far_ref):
    half = total_ref.shape[0] // shards // 2
    for owner in range(shards):
        rows = slice(owner * half, (owner + 1) * half)
        near = pl.ds(pl.multiple_of((2 * owner + which) * half, half), half)
        far = pl.ds(pl.multiple_of((2 * owner + 1 - which) * half, half), half)
        near_ref[rows, :] = total_ref[near, :].astype(bf16)
        far_ref[rows, :] = total_ref[far, :].astype(bf16)


def left_grad_kernel(shards, *refs):
    lefts, rights = refs[:4], refs[4:8]
    near_ref, far_ref, total_ref = refs[8:]
    lane = lax.rem(lax.axis_index("context"), 2)
    total_ref[...] = sum(tn(left[...], right[...]) for left, right in zip(lefts, rights))
    store_halves(lane, shards, total_ref, near_ref, far_ref)


def left_grad(shards, lefts, rights):
    rows, width = lefts[0].shape
    hidden = rights[0].shape[1]
    tile = hidden // 3
    half = width // 2
    return pl.pallas_call(
        functools.partial(left_grad_kernel, shards),
        grid=(3,),
        in_specs=[pl.BlockSpec((rows, width), lambda j: (0, 0))] * 4
        + [pl.BlockSpec((rows, tile), lambda j: (0, j))] * 4,
        out_specs=[pl.BlockSpec((half, tile), lambda j: (0, j))] * 2,
        out_shape=[jax.ShapeDtypeStruct((half, hidden), bf16)] * 2,
        scratch_shapes=[pltpu.VMEM((width, tile), f32)],
        cost_estimate=pl.CostEstimate(
            flops=rows * width * hidden, bytes_accessed=10**6, transcendentals=0
        ),
    )(*lefts, *rights)


def down_grad_kernel(shards, table, first_ref, second_ref, *refs):
    rights = refs[:4]
    near_ref, far_ref, total_ref = refs[4:]
    lane = lax.rem(lax.axis_index("context"), 2)
    tile = first_ref.shape[1]
    total = None
    for index, right in enumerate(rights):
        order = (first_ref, second_ref) if index < 2 else (second_ref, first_ref)
        for part, left in enumerate(order):
            term = tn(left[table[index]], right[part * tile : (part + 1) * tile, :])
            total = term if total is None else total + term
    total_ref[...] = total
    store_halves(lane, shards, total_ref, near_ref, far_ref)


def down_grad(shards, sequences, up_first, up_second, rights):
    rows, hidden = rights[0].shape
    width = up_first.shape[2]
    tile = hidden // 3
    half = width // 2
    whole = pl.BlockSpec(up_first.shape, lambda j, t: (0, 0, 0))
    return pl.pallas_call(
        functools.partial(down_grad_kernel, shards),
        grid_spec=pltpu.PrefetchScalarGridSpec(
            num_scalar_prefetch=1,
            grid=(3,),
            in_specs=[whole, whole] + [pl.BlockSpec((rows, tile), lambda j, t: (0, j))] * 4,
            out_specs=[pl.BlockSpec((half, tile), lambda j, t: (0, j))] * 2,
            scratch_shapes=[pltpu.VMEM((width, tile), f32)],
        ),
        out_shape=[jax.ShapeDtypeStruct((half, hidden), bf16)] * 2,
        cost_estimate=pl.CostEstimate(
            flops=rows * width * hidden, bytes_accessed=10**6, transcendentals=0
        ),
    )(sequences, up_first, up_second, *rights)


def attn_grad_kernel(shards, normed_ref, grad_ref, upstream_ref, mixed_ref, near_ref, far_ref, total_ref):
    pair = lax.axis_index("context") // 2
    columns = grad_ref.shape[1]
    total_ref[:, :columns] = tn(normed_ref[...], grad_ref[...])
    total_ref[:, columns:] = tn(upstream_ref[...], mixed_ref[...])
    store_halves(pair, shards, total_ref, near_ref, far_ref)


def attn_weight_grad(shards, normed, grad, upstream, mixed):
    width = normed.shape[1]
    columns = grad.shape[1] + mixed.shape[1]
    return pl.pallas_call(
        functools.partial(attn_grad_kernel, shards),
        in_specs=[whole_spec()] * 4,
        out_specs=[whole_spec()] * 2,
        out_shape=[jax.ShapeDtypeStruct((width // 2, columns), bf16)] * 2,
        scratch_shapes=[pltpu.VMEM((width, columns), f32)],
        cost_estimate=pl.CostEstimate(
            flops=10**8, bytes_accessed=10**6, transcendentals=0
        ),
    )(normed, grad, upstream, mixed)


def join_ffn_kernel(pieces, outs):
    context = lax.axis_index("context")
    pair, lane = context // 2, lax.rem(context, 2)
    gate_ref, up_ref, down_ref = outs
    half, columns = pieces[0][0].shape
    hidden = columns // 3
    for row in range(2):
        for column in range(2):
            for part in range(3):
                cols = slice(part * hidden, (part + 1) * hidden)
                values = [
                    jnp.where(pair == column, pieces[a][0][:, cols], pieces[a][1][:, cols])
                    for a in range(2)
                ]
                value = jnp.where(lane == row, values[0], values[1]).astype(f32)
                rows = slice(row * half, (row + 1) * half)
                into = slice(column * hidden, (column + 1) * hidden)
                if part == 2:
                    down_ref[into, rows] = value.T
                else:
                    (gate_ref, up_ref)[part][rows, into] = value


def join_ffn(near, near_pair, far, far_pair):
    half, columns = near.shape
    hidden = columns // 3

    def kernel(a, b, c, d, *outs):
        join_ffn_kernel([[a, b], [c, d]], outs)

    return pl.pallas_call(
        kernel,
        in_specs=[whole_spec()] * 4,
        out_specs=[whole_spec()] * 3,
        out_shape=[
            jax.ShapeDtypeStruct((2 * half, 2 * hidden), f32),
            jax.ShapeDtypeStruct((2 * half, 2 * hidden), f32),
            jax.ShapeDtypeStruct((2 * hidden, 2 * half), f32),
        ],
        cost_estimate=pl.CostEstimate(flops=10**6, bytes_accessed=10**6, transcendentals=0),
    )(near, near_pair, far, far_pair)


def join_attn(q_cols, kv_cols, near, near_pair, far, far_pair):
    half, columns = near.shape
    o_rows = columns - q_cols - 2 * kv_cols
    cuts = [
        slice(0, q_cols),
        slice(q_cols, q_cols + kv_cols),
        slice(q_cols + kv_cols, q_cols + 2 * kv_cols),
        slice(q_cols + 2 * kv_cols, columns),
    ]

    def kernel(a, b, c, d, q_ref, k_ref, v_ref, o_ref):
        context = lax.axis_index("context")
        pair, lane = context // 2, lax.rem(context, 2)
        for column in range(2):
            for row in range(2):
                rows = slice(row * half, (row + 1) * half)
                for part, cols in enumerate(cuts):
                    one = jnp.where(pair == row, a[:, cols], b[:, cols])
                    two = jnp.where(pair == row, c[:, cols], d[:, cols])
                    value = jnp.where(lane == column, one, two).astype(f32)
                    wide = cols.stop - cols.start
                    into = slice(column * wide, (column + 1) * wide)
                    if part == 3:
                        o_ref[into, rows] = value.T
                    else:
                        (q_ref, k_ref, v_ref)[part][rows, into] = value

    return pl.pallas_call(
        kernel,
        in_specs=[whole_spec()] * 4,
        out_specs=[whole_spec()] * 4,
        out_shape=[
            jax.ShapeDtypeStruct((2 * half, 2 * q_cols), f32),
            jax.ShapeDtypeStruct((2 * half, 2 * kv_cols), f32),
            jax.ShapeDtypeStruct((2 * half, 2 * kv_cols), f32),
            jax.ShapeDtypeStruct((2 * o_rows, 2 * half), f32),
        ],
        cost_estimate=pl.CostEstimate(flops=10**6, bytes_accessed=2 * 10**6, transcendentals=0),
    )(near, near_pair, far, far_pair)


def join_rows(places, values, out_dtype):
    block, width = values[0].shape

    def kernel(table, a, b, c, d, out_ref):
        for index, ref in enumerate((a, b, c, d)):

            @pl.when(table[index] == pl.program_id(0))
            def _():
                out_ref[0] = ref[...].astype(out_dtype)

    return pl.pallas_call(
        kernel,
        grid_spec=pltpu.PrefetchScalarGridSpec(
            num_scalar_prefetch=1,
            grid=(4,),
            in_specs=[pl.BlockSpec((block, width), lambda i, t: (0, 0))] * 4,
            out_specs=pl.BlockSpec((1, block, width), lambda i, t: (i, 0, 0)),
        ),
        out_shape=jax.ShapeDtypeStruct((4, block, width), out_dtype),
        cost_estimate=pl.CostEstimate(flops=10**6, bytes_accessed=10**6, transcendentals=0),
    )(places, *values)


def cut(value, index, size, axis):
    return lax.dynamic_slice_in_dim(value, index * size, size, axis)


def spread(first_rows, second_rows, pair, lane, side, out_dtype):
    first = turn(first_rows, pair, lane)
    second = lax.ppermute(second_rows, "context", TWIST_OUT)
    values = [first, second, side_swap(first), side_swap(second)]
    places = jnp.stack(
        [2 * lane + side, 2 * (1 - lane) + side, 2 * lane + 1 - side, 2 * (1 - lane) + 1 - side]
    ).astype(jnp.int32)
    return join_rows(places, values, out_dtype)


def on_device(
    inputs,
    lengths,
    query_weight,
    key_weight,
    value_weight,
    out_weight,
    gate_weight,
    up_weight,
    down_weight,
    norm_gains,
    head_gains,
    cotangent,
):
    block_len, width = inputs.shape[1:]
    full_len = 4 * block_len
    context = lax.axis_index("context")
    pair, lane, side = context // 2, context % 2, lax.axis_index("tensor")
    owner = lax.axis_index("dp")
    shards = lax.axis_size("dp")
    shard = width // shards
    half_shard = shard // 2
    mine = 2 * pair + side

    q_cols, kv_cols, o_rows = query_weight.shape[1] // 2, key_weight.shape[1] // 2, out_weight.shape[0] // 2
    attn_shard = row_major(
        jnp.concatenate(
            [
                cut(query_weight, lane, q_cols, 1),
                cut(key_weight, lane, kv_cols, 1),
                cut(value_weight, lane, kv_cols, 1),
                cut(out_weight, lane, o_rows, 0).T,
            ],
            axis=1,
        )
    )
    qkv_cols = q_cols + 2 * kv_cols
    attn_own = lax.all_gather(row_major(cross_swap(attn_shard, lane, side)), "dp", axis=0, tiled=True)
    qkv_own, out_own = row_major(attn_own[:, :qkv_cols]), row_major(attn_own[:, qkv_cols:])
    qkv_far, out_far = row_major(side_swap(qkv_own)), row_major(side_swap(out_own))

    gains_all = lax.all_gather(jnp.concatenate([norm_gains, head_gains], axis=1), "dp", axis=0)
    gains_full = gains_all[:, :, :shard].transpose(1, 0, 2).reshape(2, width).astype(f32)
    head_full = gains_all[:, :, shard:].transpose(1, 0, 2).reshape(2, HD).astype(f32)
    head_pair = jnp.concatenate([head_full, head_full], axis=1)
    gain_attn, gain_ffn = gains_full[0], gains_full[1]

    hidden = gate_weight.shape[1] // 2
    ffn_shard = row_major(
        jnp.concatenate(
            [
                cut(cut(gate_weight, lane, half_shard, 0), pair, hidden, 1),
                cut(cut(up_weight, lane, half_shard, 0), pair, hidden, 1),
                cut(cut(down_weight, lane, half_shard, 1), pair, hidden, 0).T,
            ],
            axis=1,
        )
    )
    ffn_own = row_major(lax.all_gather(ffn_shard, "dp", axis=0, tiled=True))

    first_in = turn(
        lax.dynamic_index_in_dim(inputs, 2 * lane + side, 0, False), pair, lane
    )
    second_in = lax.ppermute(
        lax.dynamic_index_in_dim(inputs, 2 * (1 - lane) + side, 0, False), "context", TWIST_IN
    )
    x_half = jnp.concatenate([first_in, second_in], axis=0).astype(f32)
    half_len = x_half.shape[0]

    position = context * block_len + jnp.arange(block_len, dtype=jnp.int32)
    live = position[None, :] < lengths[:, None]
    upstream_low = jnp.where(live[:, :, None], cotangent, jnp.zeros((), bf16))
    upstream_low = after(upstream_low, first_in, second_in)
    up_first = turn(upstream_low, pair, lane)
    up_second = lax.ppermute(upstream_low, "context", TWIST_IN)

    scale_one = rms_scale(x_half)
    normal_one = x_half * scale_one
    normed_half = (normal_one * gain_attn).astype(bf16)
    normed_one = jnp.concatenate([normed_half, lane_swap(normed_half)], axis=0)
    true_block = jnp.arange(4, dtype=jnp.int32)
    local_block = jnp.where(true_block // 2 == lane, 0, 2) + jnp.where(true_block % 2 == pair, 0, 1)
    table = jnp.concatenate([local_block, lax.dynamic_slice_in_dim(lengths, mine, 1)]).astype(jnp.int32)
    cosine, sine = rope_tables(full_len)
    qkv = [nn(normed_one, qkv_own), nn(normed_one, qkv_far)]
    qkv[1] = after(qkv[1], up_first, up_second)
    mixed, inverse, q_rot, k_rot = zip(
        *[attend_forward(table, value, cosine, sine, head_pair) for value in qkv]
    )
    attn_part = nt(mixed[0], out_own) + nt(mixed[1], out_far)
    attn_recv = lane_swap(attn_part[half_len:].astype(bf16))
    middle = x_half + attn_part[:half_len] + attn_recv.astype(f32)
    scale_two = rms_scale(middle)
    normal_two = middle * scale_two
    normed_a = (normal_two * gain_ffn).astype(bf16)
    ffn_own = after(ffn_own, normed_a)
    ffn_far = row_major(lane_swap(ffn_own))
    normed_b = side_swap(normed_a)
    normed_c = pair_swap(normed_a)

    far_pair = 2 * (1 - pair)
    sequences = jnp.stack(
        [mine, 2 * pair + 1 - side, far_pair + side, far_pair + 1 - side]
    ).astype(jnp.int32)

    def run(index, normed, out_dtype):
        return feed_forward(
            sequences[index], index >= 2, out_dtype, shards, normed, up_first, up_second, ffn_own, ffn_far
        )

    done_a = run(0, normed_a, f32)
    normed_b, normed_c = after(normed_b, done_a[0]), after(normed_c, done_a[0])
    normed_d = jnp.concatenate(
        [side_swap(normed_c[:block_len]), pair_swap(normed_b[block_len:])], axis=0
    )
    done_b = run(1, normed_b, bf16)
    done_d = run(3, after(normed_d, done_b[0]), bf16)
    done_c = run(2, after(normed_c, done_d[0]), bf16)

    def first_stage(which):
        return side_swap(done_d[which][block_len:]), pair_swap(done_d[which][:block_len])

    def second_stage(which, from_side, from_pair):
        b, c = done_b[which], done_c[which]
        send_b = jnp.concatenate([b[:block_len] + from_pair, b[block_len:]], axis=0)
        send_c = jnp.concatenate([c[:block_len], c[block_len:] + from_side], axis=0)
        return send_b, send_c

    back_from = first_stage(1)
    rights = [(done_a, done_b, done_c, done_d)[i][2] for i in range(4)]
    down_near, down_far = down_grad(shards, sequences, up_first, up_second, rights)
    send_b, send_c = second_stage(1, *back_from)
    lefts = [normed_a, normed_b, normed_c, normed_d]
    send_b, send_c, lefts[0], down_near = lax.optimization_barrier(
        (send_b, send_c, normed_a, down_near)
    )
    back_b, back_c = side_swap(send_b), pair_swap(send_c)
    gates = [(done_a, done_b, done_c, done_d)[i][3] for i in range(4)]
    ups = [(done_a, done_b, done_c, done_d)[i][4] for i in range(4)]
    gate_near, gate_far = left_grad(shards, lefts, gates)
    lefts[0] = after(lefts[0], gate_near)
    up_near, up_far = left_grad(shards, lefts, ups)
    ffn_sum = jnp.concatenate(
        [
            gate_near + lane_swap(gate_far),
            up_near + lane_swap(up_far),
            down_near + lane_swap(down_far),
        ],
        axis=1,
    )
    ffn_piece = row_major(lax.psum_scatter(row_major(ffn_sum), "dp", scatter_dimension=0, tiled=True))
    ffn_pair = pair_swap(ffn_piece)
    gate_shard, up_shard, down_shard = join_ffn(
        ffn_piece, ffn_pair, lane_swap(ffn_piece), lane_swap(ffn_pair)
    )

    upstream = jnp.concatenate(
        [
            lax.dynamic_index_in_dim(up_first, mine, 0, False),
            lax.dynamic_index_in_dim(up_second, mine, 0, False),
        ],
        axis=0,
    ).astype(f32)
    back_two = done_a[1] + back_b.astype(f32) + back_c.astype(f32)
    gain_ffn_grad = jnp.sum(back_two * normal_two, axis=0)
    middle_grad = upstream + norm_back(back_two * gain_ffn, normal_two, scale_two)
    feed_from = first_stage(0)
    send_b, send_c = second_stage(0, *feed_from)
    send_b, send_c = after(send_b, back_two), after(send_c, back_two)
    feed_sum = done_a[0] + side_swap(send_b).astype(f32) + pair_swap(send_c).astype(f32)
    out_half = (middle + feed_sum).astype(bf16)

    attn_low = after(middle_grad.astype(bf16), up_near)
    attn_grad = jnp.concatenate([attn_low, lane_swap(attn_low)], axis=0)
    weights = [(qkv_own, out_own), (qkv_far, out_far)]
    pieces, back_one, gain_parts = {}, None, 0.0
    for which in (1, 0):
        mixed_grad = nn(attn_grad, weights[which][1]).astype(bf16)
        if which == 0:
            mixed_grad = after(mixed_grad, pieces[1][0], send_b, send_c)
        qkv_grad, gain_part = attend_backward(
            table,
            qkv[which],
            cosine,
            sine,
            head_pair,
            q_rot[which],
            k_rot[which],
            mixed[which],
            inverse[which],
            mixed_grad,
        )
        pieces[which] = attn_weight_grad(shards, normed_one, qkv_grad, attn_grad, mixed[which])
        term = nt(qkv_grad, weights[which][0])
        back_one = term if back_one is None else back_one + term
        gain_parts = gain_parts + gain_part
    back_recv = lane_swap(back_one[half_len:].astype(bf16))
    back_half = back_one[:half_len] + back_recv.astype(f32)
    gain_attn_grad = jnp.sum(back_half * normal_one, axis=0)
    outputs = spread(out_half[:block_len], out_half[block_len:], pair, lane, side, bf16)
    back_half = after(back_half, out_half)
    input_half = (middle_grad + norm_back(back_half * gain_attn, normal_one, scale_one)).astype(bf16)
    input_grad = spread(input_half[:block_len], input_half[block_len:], pair, lane, side, f32)

    near, far = (mine_part + side_swap(other) for mine_part, other in zip(pieces[0], pieces[1]))
    attn_sum = row_major(near + pair_swap(far))
    attn_piece = row_major(lax.psum_scatter(attn_sum, "dp", scatter_dimension=0, tiled=True))
    attn_piece = cross_swap(attn_piece, lane, side)
    piece_pair = pair_swap(attn_piece)
    query_shard, key_shard, value_shard, out_shard = join_attn(
        q_cols, kv_cols, attn_piece, piece_pair, lane_swap(attn_piece), lane_swap(piece_pair)
    )

    head_grad = gain_parts[:2, :HD] + gain_parts[:2, HD:]
    gain_total = jnp.concatenate([jnp.stack([gain_attn_grad, gain_ffn_grad]), head_grad], axis=1)
    gain_total = gain_total + lane_swap(gain_total)
    gain_total = gain_total + side_swap(gain_total)
    gain_total = gain_total + pair_swap(gain_total)
    hop = 1
    while hop < shards:
        pairs = [(i, i ^ hop) for i in range(shards)]
        gain_total = gain_total + lax.ppermute(gain_total, "dp", pairs)
        hop *= 2
    gain_shard = cut(gain_total[:, :width], owner, shard, 1)
    head_shard = cut(gain_total[:, width:], owner, HD // shards, 1)
    return (
        outputs,
        input_grad,
        query_shard,
        key_shard,
        value_shard,
        out_shard,
        gate_shard,
        up_shard,
        down_shard,
        gain_shard,
        head_shard,
    )


def solution(mesh):
    in_specs = (
        P("dp", "context", None),
        P("dp"),
        P("dp", "tensor"),
        P("dp", "tensor"),
        P("dp", "tensor"),
        P("tensor", "dp"),
        P("dp", "tensor"),
        P("dp", "tensor"),
        P("tensor", "dp"),
        P(None, "dp"),
        P(None, "dp"),
        P("dp", "context", None),
    )
    out_specs = (
        P("dp", "context", None),
        P("dp", "context", None),
        P("dp", "tensor"),
        P("dp", "tensor"),
        P("dp", "tensor"),
        P("tensor", "dp"),
        P("dp", "tensor"),
        P("dp", "tensor"),
        P("tensor", "dp"),
        P(None, "dp"),
        P(None, "dp"),
    )
    return jax.shard_map(
        on_device, mesh=mesh, in_specs=in_specs, out_specs=out_specs, check_vma=False
    )
```
